32 devices in a mesh: dir: 8 (over z, y), near: 4 (over x, core).
Axes of the slice: x: 2, y: 2, z: 4, core: 2. Of those that a mesh axis runs over, the one named last changes fastest.
Arguments:
- currents: bfloat16 [1024, 128, 128], P(('dir', 'near')), may hold values from -6 to 6
- counts: int32 [32], replicated, may hold values from 0 to 4, as said below
- near_source: int32 [1024, 6], P(('dir', 'near')), may hold values from 0 to 1023, as said below
- near_blocks: bfloat16 [1024, 6, 128, 256], P(('dir', 'near')), may hold values from -0.15625 to 0.15625
- aggregate: bfloat16 [8, 1152, 256], replicated, may hold values from -0.125 to 0.125
- receive: bfloat16 [8, 128, 2304], replicated, may hold values from -0.125 to 0.125
- translations: bfloat16 [1, 1, 1152, 64, 128], P(None, None, ('dir', 'near')), may hold values from -0.5 to 0.5
- source_blocks: int32 [1, 1], replicated, may hold values from 0 to 0, as said below
Outputs:
- fields: bfloat16 [1024, 128, 128], P(('dir', 'near'))
The draws below stay inside these ranges and needn't reach their ends.
Inputs may be any that keep to these rules, and one draw needn't show every extreme that they name: `counts`: devices 2 m and 2 m + 1 of dir and near together (neighbours along near) own exactly 4 parents between them; some device owns 4 and its neighbour none. `near_source`: every entry names a live leaf slot on the device of its row or on a device next to it along near with the same dir index. `source_blocks`: each row names 1 different blocks.
All inputs are finite; a program needn't handle non-finite values.
Results may differ from the reference program's by a relative error of at most 0.005.
Values may be sent and summed in bfloat16 or wider, within the bound.
A program may use at most 128 MiB of HBM per device.

```python
import jax
import jax.numpy as jnp
from jax import lax

P_SIZE = 128
R = 64
K = 1152
NEAR_PER = 6
PAR_SLOTS = 4
BLOCK = 64
PARENTS = 64
LEAF_SLOTS = 32
NBLK = 1
LIST = 1
N_NEAR = 4
DEVICES = 32


def owned_counts(key):
    pair_count = PARENTS // PAR_SLOTS
    first_share = jax.random.randint(jax.random.fold_in(key, 11), (pair_count,), 0, PAR_SLOTS + 1)
    chosen = jax.random.randint(jax.random.fold_in(key, 12), (), 0, pair_count)
    extreme = PAR_SLOTS * jax.random.randint(jax.random.fold_in(key, 13), (), 0, 2)
    first_share = jnp.where(jnp.arange(pair_count) == chosen, extreme, first_share)
    return jnp.stack([first_share, PAR_SLOTS - first_share], axis=1).reshape(-1).astype(jnp.int32)


def draw_counts(key, part):
    return owned_counts(key)


def draw_near_source(key, part):
    counts = owned_counts(key)
    devices = counts.shape[0]
    slot_rows = devices * LEAF_SLOTS
    home_device = jnp.arange(slot_rows, dtype=jnp.int32) // LEAF_SLOTS
    shifts = jnp.array([-1, 0, 1], jnp.int32)
    position = home_device % N_NEAR
    moved_position = position[:, None] + shifts[None, :]
    inside = (moved_position >= 0) & (moved_position < N_NEAR)
    target = jnp.clip(home_device[:, None] + shifts[None, :], 0, devices - 1)
    has_parents = counts[target] > 0
    allowed = inside & has_parents
    scores = jax.random.randint(jax.random.fold_in(key, 21), (slot_rows, NEAR_PER, 3), 0, 1024) * 4 + jnp.arange(3, dtype=jnp.int32)
    scores = jnp.where(allowed[:, None, :], scores, -1)
    picked = jnp.argmax(scores, axis=-1)
    chosen = jnp.take_along_axis(jnp.broadcast_to(target[:, None, :], scores.shape), picked[..., None], axis=-1)[..., 0]
    slot_limit = 8 * counts[chosen]
    slot_drawn = jax.random.randint(jax.random.fold_in(key, 22), (slot_rows, NEAR_PER), 0, slot_limit)
    return (chosen * LEAF_SLOTS + slot_drawn).astype(jnp.int32)


def draw_source_blocks(key, part):
    scores = jax.random.randint(jax.random.fold_in(key, 31), (NBLK, NBLK), 0, 4096) * NBLK + jnp.arange(NBLK, dtype=jnp.int32)[None, :]
    ranked = jnp.argsort(scores, axis=1)
    return ranked[:, :LIST].astype(jnp.int32)


def shard_levels(key, extent, pieces, smallest, top_value):
    gain, own = 1.0, jax.random.fold_in(key, 6)
    for dim, blocks in pieces:
        draws = jnp.exp(jax.random.uniform(jax.random.fold_in(own, dim), (blocks,), jnp.float32, smallest / len(pieces), top_value / len(pieces)))
        gain = gain * jnp.repeat(draws, extent[dim] // blocks).reshape([-1 if axis == dim else 1 for axis in range(len(extent))])
    return gain


def scatter_about(key, shape, width, reach, pieces=(), kind=jnp.bfloat16):
    gain = shard_levels(key, shape, pieces, -0.22, 0.18) if pieces else 1.0
    drawn = jax.random.normal(key, shape, jnp.float32) * width * gain
    return jnp.minimum(jnp.maximum(drawn, -reach), reach).astype(kind)


def setup_inputs(seed: int = 0) -> dict:
    arg_keys = jax.random.split(jax.random.key(seed), 9)
    currents = scatter_about(arg_keys[0], (DEVICES * LEAF_SLOTS, P_SIZE, 2 * R), 1.0, 6.0, ((0, 32),))
    counts = draw_counts(jax.random.fold_in(arg_keys[8], 71), 0)
    near_source = draw_near_source(jax.random.fold_in(arg_keys[8], 71), 0)
    near_blocks = scatter_about(arg_keys[3], (DEVICES * LEAF_SLOTS, NEAR_PER, P_SIZE, 2 * P_SIZE), (2 * P_SIZE * NEAR_PER) ** -0.5, 0.15625, ((0, 32),))
    aggregate = scatter_about(arg_keys[4], (8, K, 2 * P_SIZE), (16 * P_SIZE) ** -0.5, 0.125)
    receive = scatter_about(arg_keys[5], (8, P_SIZE, 2 * K), (2 * K) ** -0.5, 0.125)
    translations = scatter_about(arg_keys[6], (NBLK, LIST, K, BLOCK, 2 * BLOCK), (2 * BLOCK * LIST) ** -0.5, 0.5, ((2, 32),))
    source_blocks = draw_source_blocks(jax.random.fold_in(arg_keys[8], 71), 0)
    return {"currents": currents, "counts": counts, "near_source": near_source, "near_blocks": near_blocks, "aggregate": aggregate, "receive": receive, "translations": translations, "source_blocks": source_blocks}


def turned(values):
    middle = values.shape[-1] // 2
    return jnp.concatenate([-values[..., middle:], values[..., :middle]], axis=-1)


def parent_positions(counts):
    range_ends = jnp.cumsum(counts).astype(jnp.int32)
    parent_ids = jnp.arange(PARENTS, dtype=jnp.int32)
    before = (range_ends[None, :] <= parent_ids[:, None]).astype(jnp.int32)
    owners = jnp.sum(before, axis=1).astype(jnp.int32)
    starts = jnp.sum(before * counts[None, :], axis=1).astype(jnp.int32)
    return (owners * PAR_SLOTS + parent_ids - starts).astype(jnp.int32)


def reference(currents, counts, near_source, near_blocks, aggregate, receive, translations, source_blocks):
    slots = parent_positions(counts)
    leaves = currents.reshape(-1, 8, P_SIZE, 2 * R)
    owned = leaves[slots]
    stacked = jnp.concatenate([owned, turned(owned)], axis=2)
    aggregate_wide = aggregate.astype(jnp.float32)

    def radiate(group_rows):
        return jnp.einsum("ckq,gcqr->gkr", aggregate_wide, group_rows.astype(jnp.float32)).astype(jnp.bfloat16)

    patterns = lax.map(radiate, stacked.reshape(-1, 8, 8, 2 * P_SIZE, 2 * R)).reshape(PARENTS, K, 2 * R)
    blocks = patterns.reshape(NBLK, BLOCK, K, 2 * R)
    with_turned = jnp.concatenate([blocks, turned(blocks)], axis=1)

    def translate(target):
        sources = with_turned[source_blocks[target]].astype(jnp.float32)
        operators = translations[target].astype(jnp.float32)
        return jnp.einsum("lkij,ljkr->ikr", operators, sources).astype(jnp.bfloat16)

    incoming = lax.map(translate, jnp.arange(NBLK, dtype=jnp.int32)).reshape(PARENTS, K, 2 * R)
    receive_wide = receive.astype(jnp.float32)

    def absorb(group_rows):
        doubled = jnp.concatenate([group_rows, turned(group_rows)], axis=1).astype(jnp.float32)
        return jnp.einsum("cpk,gkr->gcpr", receive_wide, doubled)

    far_field = lax.map(absorb, incoming.reshape(-1, 8, K, 2 * R)).reshape(PARENTS * 8, P_SIZE, 2 * R)
    leaf_ids = (slots[:, None] * 8 + jnp.arange(8, dtype=jnp.int32)[None, :]).reshape(-1).astype(jnp.int32)

    def nearby(indices):
        operators = near_blocks[indices].astype(jnp.float32)
        sources = currents[near_source[indices]]
        doubled = jnp.concatenate([sources, turned(sources)], axis=2).astype(jnp.float32)
        return jnp.einsum("genq,geqr->gnr", operators, doubled)

    near_field = lax.map(nearby, leaf_ids.reshape(-1, 64)).reshape(-1, P_SIZE, 2 * R)
    summed = (far_field + near_field).astype(jnp.bfloat16)
    return jnp.zeros(currents.shape, jnp.bfloat16).at[leaf_ids].set(summed)
```

```python
import functools

import jax
import jax.numpy as jnp
from jax import lax
from jax.experimental import pallas as pl
from jax.experimental.pallas import tpu as pltpu
from jax.sharding import PartitionSpec as P

MESH = pl.DeviceIdType.MESH
F32 = jnp.float32
BF16 = jnp.bfloat16
CHILDREN = 8


def turned(values):
    width = values.shape[-1]
    rolled = pltpu.roll(values, width // 2, values.ndim - 1)
    lane = lax.broadcasted_iota(jnp.int32, values.shape, values.ndim - 1)
    return jnp.where(lane < width // 2, -rolled, rolled)


def flipped(index, step, count):
    total = 0
    bit = 1
    while bit < count:
        total = total + bit * lax.rem(index // bit + step // bit, 2)
        bit *= 2
    return total


def chunks_of(per, slots):
    pieces = max(1, min(3, per // 4))
    base = per if pieces == 1 else per // pieces // 4 * 4
    sizes = [base] * (pieces - 1)
    sizes.append(per - sum(sizes))
    out, first = [], 0
    for size in sizes:
        out.append((first, size, -(-size * slots // 8) * 8 // slots))
        first += size
    return tuple(out)


def kernel(dims, counts, near_source, source_blocks, currents, near_blocks, aggregate, receive, translations, out, *scratch):
    dirs, nears, per, slots, chunks, tiles = dims
    devices = dirs * nears
    pieces = len(chunks)
    (
        pool,
        window,
        near_v,
        agg_v,
        rec_v,
        tra_v,
        stack,
        tile_rows,
        joined,
        fields,
        rec_last,
        fields_last,
        far_acc,
        far_own,
        far_send,
        far_recv,
        near_acc,
        load_sem,
        pair_sem,
        halo_sem,
        a2a_sem,
        far_sem,
    ) = scratch[:22]
    rest = scratch[22:]
    packs, send1, recv1, gathered, incoming, send2, recv2, spread = (
        rest[i * pieces : (i + 1) * pieces] for i in range(8)
    )
    leaf_slots, unknowns, channels = out.shape
    parent_slots = leaf_slots // CHILDREN
    half = parent_slots // 2
    near_per = near_v.shape[1]
    directions = agg_v.shape[1]
    dir_index = lax.axis_index("dir")
    near_index = lax.axis_index("near")
    me = dir_index * nears + near_index
    odd = lax.rem(near_index, 2)
    mate = near_index + 1 - 2 * odd
    half_leaves = half * CHILDREN
    own = pool.at[pl.ds(0, leaf_slots)]
    borrowed = pool.at[pl.ds(leaf_slots, half_leaves)]

    def deltas(index, count):
        steps, bit = [], 1
        while bit < count:
            steps.append((bit, bit - 2 * bit * lax.rem(index // bit, 2)))
            bit *= 2
        return steps

    dir_deltas, near_deltas = deltas(dir_index, dirs), deltas(near_index, nears)

    def partner(step):
        d, n = dir_index, near_index
        for bit, delta in dir_deltas:
            if step // nears & bit:
                d = d + delta
        for bit, delta in near_deltas:
            if step % nears & bit:
                n = n + delta
        return d, n

    load_own = pltpu.make_async_copy(currents, own, load_sem.at[0])
    load_agg = pltpu.make_async_copy(aggregate, agg_v, load_sem.at[1])
    load_mid = pltpu.make_async_copy(currents, window.at[pl.ds(leaf_slots, leaf_slots)], load_sem.at[2])
    load_tra = pltpu.make_async_copy(translations, tra_v, load_sem.at[3])
    load_rec = pltpu.make_async_copy(receive, rec_v, load_sem.at[4])
    load_near = pltpu.make_async_copy(near_blocks, near_v, load_sem.at[5])

    def start_pieces(source, target, sem, count):
        size = target.shape[0] // count
        for piece in range(count):
            cut = pl.ds(piece * size, size)
            pltpu.make_async_copy(source.at[cut], target.at[cut], sem).start()

    load_own.start()
    start_pieces(aggregate, agg_v, load_sem.at[1], 8)
    load_tra.start()
    start_pieces(receive, rec_v, load_sem.at[4], 8)
    load_mid.start()
    start_pieces(near_blocks, near_v, load_sem.at[5], 8)

    barrier = pltpu.get_barrier_semaphore()
    for step in range(1, devices):
        pl.semaphore_signal(barrier, inc=1, device_id=partner(step), device_id_type=MESH)
    pl.semaphore_wait(barrier, devices - 1)

    to_mate = pltpu.make_async_remote_copy(
        src_ref=currents.at[pl.ds((1 - odd) * half_leaves, half_leaves)],
        dst_ref=borrowed,
        send_sem=pair_sem.at[0],
        recv_sem=pair_sem.at[1],
        device_id=(dir_index, mate),
        device_id_type=MESH,
    )
    to_mate.start()

    own_count = counts[me]
    mate_count = counts[dir_index * nears + mate]
    even_count = jnp.where(odd == 0, own_count, mate_count)
    load_own.wait()
    to_mate.wait_recv()
    for w in range(half):
        is_own = jnp.where(odd == 0, w < own_count, half + w >= even_count)
        own_slot = jnp.clip(jnp.where(odd == 0, w, half + w - even_count), 0, parent_slots - 1)
        mate_slot = jnp.clip(jnp.where(odd == 0, w - own_count, w), 0, half - 1)
        slot = jnp.where(is_own, own_slot, parent_slots + mate_slot)
        for c in range(CHILDREN):
            values = pool[slot * CHILDREN + c]
            lanes = pl.ds(w * channels, channels)
            stack[pl.ds(2 * c * unknowns, unknowns), lanes] = values
            stack[pl.ds((2 * c + 1) * unknowns, unknowns), lanes] = turned(values.astype(F32)).astype(BF16)
    load_agg.wait()

    def hop(buffer, target, index, to, phase, p):
        return pltpu.make_async_remote_copy(
            src_ref=buffer.at[index],
            dst_ref=target.at[me],
            send_sem=a2a_sem.at[phase, p, 0],
            recv_sem=a2a_sem.at[phase, p, 1],
            device_id=to,
            device_id_type=MESH,
        )

    def all_moved(buffer, phase, p, which):
        some = buffer.at[pl.ds(0, devices - 1)]
        pltpu.make_async_copy(some, some, a2a_sem.at[phase, p, which]).wait()

    tile_devices = devices // tiles
    tile_dirs = tile_devices // nears
    rows = tile_devices * per
    my_tile = dir_index // tile_dirs

    def radiate(tile):
        start = pl.multiple_of(tile * rows, 16)
        left = jnp.concatenate([agg_v[c, pl.ds(start, rows), :] for c in range(CHILDREN)], axis=1)
        result = jnp.dot(left, stack[...], preferred_element_type=F32)
        for s in range(slots):
            tile_rows[s] = result[:, s * channels : (s + 1) * channels]

    def pack(tile, p):
        first, size, padded = chunks[p]
        for q in range(tile_devices):
            for s in range(slots):
                packs[p][pl.ds((q * slots + s) * padded, size), :] = tile_rows[s, pl.ds(q * per + first, size), :]
        shape = (tile_devices,) + send1[p].shape[1:]
        send1[p][pl.ds(tile * tile_devices, tile_devices)] = packs[p][...].reshape(shape).astype(BF16)

    def radiate_and_send(step, carry):
        tile = flipped(my_tile, tiles - 1 - step, tiles)
        radiate(tile)
        pack(tile, 0)
        for q in range(tile_devices):
            d, n = partner(q)
            d = d + (tile - my_tile) * tile_dirs
            hop(send1[0], recv1[0], d * nears + n, (d, n), 0, 0).start()
        for p in range(1, pieces):
            pack(tile, p)
        return carry

    lax.fori_loop(0, tiles - 1, radiate_and_send, 0)
    radiate(my_tile)
    pack(my_tile, 0)
    for q in range(1, tile_devices):
        d, n = partner(q)
        hop(send1[0], recv1[0], d * nears + n, (d, n), 0, 0).start()
    for p in range(1, pieces):
        pack(my_tile, p)
        for step in range(devices - 1, 0, -1):
            d, n = partner(step)
            hop(send1[p], recv1[p], d * nears + n, (d, n), 0, p).start()

    def halo(side, block):
        return pltpu.make_async_remote_copy(
            src_ref=currents,
            dst_ref=window.at[pl.ds(block * leaf_slots, leaf_slots)],
            send_sem=halo_sem.at[0, block // 2],
            recv_sem=halo_sem.at[1, block // 2],
            device_id=(dir_index, near_index + side),
            device_id_type=MESH,
        )

    @pl.when(near_index < nears - 1)
    def _():
        halo(1, 0).start()

    @pl.when(near_index > 0)
    def _():
        halo(-1, 2).start()

    for p in range(pieces):
        recv1[p][me] = send1[p][me]
    joined[...] = jnp.zeros_like(joined)

    load_rec.wait()
    last_first, last_size, _ = chunks[-1]
    last_total = devices * last_size
    for o in range(last_total // 128):
        ends = [(i // last_size) * per + last_first + i % last_size for i in (o * 128, o * 128 + 127)]
        low, high = ends[0] // 128 * 128, (ends[1] // 128 + 1) * 128
        row = lax.broadcasted_iota(jnp.int32, (high - low, 128), 0) + low
        column = lax.broadcasted_iota(jnp.int32, (high - low, 128), 1) + o * 128
        owner = (row * (2**16 // per + 1)) >> 16
        place = row - owner * per - last_first
        chosen = (place >= 0) & (place < last_size) & (owner * last_size + place == column)
        chooser = jnp.where(chosen, 1.0, 0.0).astype(BF16)
        for part in range(2):
            left = rec_v[:, :, pl.ds(part * directions + low, high - low)].reshape(CHILDREN * unknowns, high - low)
            picked = jnp.dot(left, chooser, preferred_element_type=F32).astype(BF16)
            rec_last[:, pl.ds(part * last_total + o * 128, 128)] = picked

    load_tra.wait()
    blocks, listed, _, block_size, doubled = tra_v.shape
    per_block = devices // blocks
    for p in range(pieces):
        first, size, padded = chunks[p]
        message = send1[p].shape[1:]
        all_moved(recv1[p], 0, p, 1)
        for b in range(blocks):
            got = recv1[p][pl.ds(b * per_block, per_block)].astype(F32)
            gathered[p][b] = got.reshape(gathered[p].shape[1:])
        for k in range(size):
            for b in range(blocks):
                summed = None
                for l in range(listed):
                    source = 0 if blocks == 1 else source_blocks[b, l]
                    rows_k = gathered[p][source, pl.ds(k, block_size, stride=padded), :]
                    both = jnp.concatenate([rows_k, turned(rows_k)], axis=0).astype(BF16)
                    part = jnp.dot(tra_v[b, l, first + k], both, preferred_element_type=F32)
                    summed = part if summed is None else summed + part
                incoming[p][b, pl.ds(k, block_size, stride=padded), :] = summed
        for b in range(blocks):
            packed = incoming[p][b].reshape((per_block,) + message)
            send2[p][pl.ds(b * per_block, per_block)] = packed.astype(BF16)
        for step in range(devices - 1, 0, -1):
            d, n = partner(step)
            hop(send2[p], recv2[p], d * nears + n, (d, n), 1, p).start()
        recv2[p][me] = send2[p][me]

    load_mid.wait()
    load_near.wait()

    @pl.when(near_index > 0)
    def _():
        halo(1, 0).wait_recv()

    @pl.when(near_index < nears - 1)
    def _():
        halo(-1, 2).wait_recv()

    base = (me - 1) * leaf_slots
    together = 4 if leaf_slots % 4 == 0 else 1

    def nearby(step, carry):
        for u in range(together):
            i = step * together + u
            rows_at = [near_source[e, i] - base for e in range(near_per)]
            sources = [window[jnp.clip(r, 0, 3 * leaf_slots - 1)] for r in rows_at]
            parts = [near_v[i, e] for e in range(near_per)]
            real = jnp.concatenate([p[:, :unknowns] for p in parts], axis=1)
            imag = jnp.concatenate([p[:, unknowns:] for p in parts], axis=1)
            result = jnp.dot(
                jnp.concatenate([real, imag], axis=0),
                jnp.concatenate(sources, axis=0),
                preferred_element_type=F32,
            )
            near_acc[i] = result[:unknowns] + turned(result[unknowns:])
        return carry

    lax.fori_loop(0, leaf_slots // together, nearby, 0)

    for p in range(pieces - 1):
        first, size, padded = chunks[p]
        all_moved(recv2[p], 1, p, 1)
        spread[p][...] = recv2[p][...].astype(F32).reshape(spread[p].shape)
        for d in range(devices):
            for s in range(slots):
                joined[s, pl.ds(d * per + first, size), :] = spread[p][pl.ds((d * slots + s) * padded, size), :]

    def fill(target, source, total):
        for s in range(slots):
            lanes = pl.ds(s * channels, channels)
            values = source[s]
            target[pl.ds(0, total), lanes] = values.astype(BF16)
            target[pl.ds(total, total), lanes] = turned(values).astype(BF16)

    group = 2

    if pieces > 1:
        fill(fields, joined, directions)

        def absorb_most(step, carry):
            left = rec_v[pl.ds(step * group, group)].reshape(group * unknowns, 2 * directions)
            start = pl.multiple_of(step * group * unknowns, group * unknowns)
            far_acc[pl.ds(start, group * unknowns), :] = jnp.dot(left, fields[...], preferred_element_type=F32)
            return carry

        lax.fori_loop(0, CHILDREN // group, absorb_most, 0)
    else:
        far_acc[...] = jnp.zeros_like(far_acc)

    p = pieces - 1
    first, size, padded = chunks[p]
    all_moved(recv2[p], 1, p, 1)
    spread[p][...] = recv2[p][...].astype(F32).reshape(spread[p].shape)
    for d in range(devices):
        for s in range(slots):
            joined[s, pl.ds(d * size, size), :] = spread[p][pl.ds((d * slots + s) * padded, size), :]
    fill(fields_last, joined.at[:, pl.ds(0, last_total)], last_total)

    def far_copy(c):
        return pltpu.make_async_remote_copy(
            src_ref=far_send.at[c],
            dst_ref=far_recv.at[c],
            send_sem=far_sem.at[0, c],
            recv_sem=far_sem.at[1, c],
            device_id=(dir_index, mate),
            device_id_type=MESH,
        )

    def absorb(step, carry):
        start = pl.multiple_of(step * group * unknowns, group * unknowns)
        far = far_acc[pl.ds(start, group * unknowns), :] + jnp.dot(
            rec_last[pl.ds(start, group * unknowns), :], fields_last[...], preferred_element_type=F32
        )
        for u in range(group):
            c = step * group + u
            for s in range(slots):
                piece = far[u * unknowns : (u + 1) * unknowns, s * channels : (s + 1) * channels]
                far_own[c, s] = piece
                far_send[c, s] = piece.astype(BF16)
            far_copy(c).start()
        return carry

    lax.fori_loop(0, CHILDREN // group, absorb, 0)

    def finish(c, carry):
        far_copy(c).wait_recv()
        for s in range(parent_slots):
            place = jnp.where(odd == 0, s, even_count + s)
            mine_at = place - half * odd
            mine = (mine_at >= 0) & (mine_at < half)
            own_at = jnp.clip(mine_at, 0, half - 1)
            mate_at = jnp.clip(place - half * (1 - odd), 0, half - 1)
            theirs = far_recv[c, 0]
            for w in range(1, half):
                theirs = jnp.where(mate_at == w, far_recv[c, w], theirs)
            far = jnp.where(mine, far_own[c, own_at], theirs.astype(F32))
            total = far + near_acc[s * CHILDREN + c]
            out[s * CHILDREN + c] = jnp.where(s < own_count, total, 0.0).astype(BF16)
        return carry

    lax.fori_loop(0, CHILDREN, finish, 0)

    to_mate.wait_send()
    for p in range(pieces):
        all_moved(send1[p], 0, p, 0)
        all_moved(send2[p], 1, p, 0)
    for c in range(CHILDREN):
        far_copy(c).wait_send()

    @pl.when(near_index < nears - 1)
    def _():
        halo(1, 0).wait_send()

    @pl.when(near_index > 0)
    def _():
        halo(-1, 2).wait_send()


def body(
    currents, counts, near_source, near_blocks, aggregate, receive, translations, source_blocks
):
    dirs, nears = lax.axis_size("dir"), lax.axis_size("near")
    devices = dirs * nears
    leaf_slots, unknowns, channels = currents.shape
    parent_slots = leaf_slots // CHILDREN
    slots = parent_slots // 2
    blocks, listed, per, block_size, doubled = translations.shape
    directions = aggregate.shape[1]
    chunks = chunks_of(per, slots)
    tiles = 4 if dirs % 4 == 0 and directions % 64 == 0 else 1
    tile_devices = devices // tiles
    lanes = slots * channels
    last_total = devices * chunks[-1][1]
    hbm_spec = pl.BlockSpec(memory_space=pltpu.HBM)
    smem_spec = pl.BlockSpec(memory_space=pltpu.SMEM)
    messages = [(devices, slots * padded // 8, 8, channels) for _, _, padded in chunks]
    exchange = [pltpu.VMEM(m, BF16) for m in messages]
    boxes = [pltpu.VMEM((blocks, block_size * padded, channels), F32) for _, _, padded in chunks]
    scratch = [
        pltpu.VMEM((leaf_slots + slots * CHILDREN, unknowns, channels), BF16),
        pltpu.VMEM((3 * leaf_slots, unknowns, channels), BF16),
        pltpu.VMEM(near_blocks.shape, BF16),
        pltpu.VMEM(aggregate.shape, BF16),
        pltpu.VMEM(receive.shape, BF16),
        pltpu.VMEM(translations.shape, BF16),
        pltpu.VMEM((2 * CHILDREN * unknowns, lanes), BF16),
        pltpu.VMEM((slots, tile_devices * per, channels), F32),
        pltpu.VMEM((slots, directions, channels), F32),
        pltpu.VMEM((2 * directions, lanes), BF16),
        pltpu.VMEM((CHILDREN * unknowns, 2 * last_total), BF16),
        pltpu.VMEM((2 * last_total, lanes), BF16),
        pltpu.VMEM((CHILDREN * unknowns, lanes), F32),
        pltpu.VMEM((CHILDREN, slots, unknowns, channels), F32),
        pltpu.VMEM((CHILDREN, slots, unknowns, channels), BF16),
        pltpu.VMEM((CHILDREN, slots, unknowns, channels), BF16),
        pltpu.VMEM((leaf_slots, unknowns, channels), F32),
        pltpu.SemaphoreType.DMA((6,)),
        pltpu.SemaphoreType.DMA((2,)),
        pltpu.SemaphoreType.DMA((2, 2)),
        pltpu.SemaphoreType.DMA((2, len(chunks), 2)),
        pltpu.SemaphoreType.DMA((2, CHILDREN)),
    ]
    scratch += [pltpu.VMEM((tile_devices * slots * padded, channels), F32) for _, _, padded in chunks]
    scratch += exchange + exchange + boxes + boxes + exchange + exchange
    scratch += [pltpu.VMEM((devices * slots * padded, channels), F32) for _, _, padded in chunks]
    return pl.pallas_call(
        functools.partial(kernel, (dirs, nears, per, slots, chunks, tiles)),
        out_shape=jax.ShapeDtypeStruct(currents.shape, BF16),
        in_specs=[smem_spec] * 3 + [hbm_spec] * 5,
        out_specs=pl.BlockSpec(memory_space=pltpu.VMEM),
        scratch_shapes=scratch,
        compiler_params=pltpu.CompilerParams(
            collective_id=0, has_side_effects=True, vmem_limit_bytes=50 * 2**20
        ),
    )(
        counts,
        near_source.T,
        source_blocks,
        currents,
        near_blocks,
        aggregate,
        receive,
        translations,
    )


def solution(mesh):
    return jax.shard_map(
        body,
        mesh=mesh,
        in_specs=(
            P(("dir", "near"), None, None),
            P(),
            P(("dir", "near"), None),
            P(("dir", "near"), None, None, None),
            P(),
            P(),
            P(None, None, ("dir", "near"), None, None),
            P(),
        ),
        out_specs=P(("dir", "near"), None, None),
        check_vma=False,
    )
```

```python
import functools

import jax
import jax.numpy as jnp
from jax import lax
from jax.experimental import pallas as pl
from jax.experimental.pallas import tpu as pltpu
from jax.sharding import PartitionSpec as P

MESH = pl.DeviceIdType.MESH
F32 = jnp.float32
BF16 = jnp.bfloat16
CHILDREN = 8


def turned(values):
    width = values.shape[-1]
    rolled = pltpu.roll(values, width // 2, values.ndim - 1)
    lane = lax.broadcasted_iota(jnp.int32, values.shape, values.ndim - 1)
    return jnp.where(lane < width // 2, -rolled, rolled)


def flipped(index, step, count):
    total = 0
    bit = 1
    while bit < count:
        total = total + bit * lax.rem(index // bit + step // bit, 2)
        bit *= 2
    return total


SHARES = (12, 12, 12)
HALO = (4, 6, 6)


def chunks_of(per, slots):
    sizes = [per * share // sum(SHARES) // 4 * 4 for share in SHARES[:-1]]
    sizes = [size for size in sizes if size]
    sizes.append(per - sum(sizes))
    out, first = [], 0
    for size in sizes:
        out.append((first, size, -(-size * slots // 8) * 8 // slots))
        first += size
    return tuple(out)


def halo_parts_of(leaf_slots, pieces):
    sizes = [HALO[i] * leaf_slots // 32 if i < len(HALO) else 0 for i in range(pieces)]
    sizes.append(leaf_slots - sum(sizes))
    return tuple((sum(sizes[:i]), size) for i, size in enumerate(sizes))


def kernel(dims, *refs):
    dirs, nears, per, slots, chunks, halo_parts, tiles, listing = dims
    devices = dirs * nears
    pieces = len(chunks)
    source_blocks, refs = (refs[0], refs[1:]) if listing else (None, refs)
    counts_hbm, near_source_hbm, currents, near_blocks, aggregate, receive, translations, out = refs[:8]
    scratch = refs[8:]
    (
        pool,
        window,
        near_v,
        agg_v,
        rec_v,
        tra_v,
        stack,
        tile_rows,
        joined,
        fields,
        rec_last,
        fields_last,
        far_acc,
        far_own,
        far_send,
        far_recv,
        near_acc,
        load_sem,
        agg_sem,
        pair_sem,
        halo_sem,
        a2a_sem,
        far_sem,
        met_sem,
        counts,
        near_source,
        small_sem,
    ) = scratch[:27]
    rest = scratch[27:]
    packs, send1, recv1, gathered, incoming, send2, recv2, spread = (
        rest[i * pieces : (i + 1) * pieces] for i in range(8)
    )
    leaf_slots, unknowns, channels = out.shape
    parent_slots = leaf_slots // CHILDREN
    half = parent_slots // 2
    near_per = near_v.shape[1]
    directions = agg_v.shape[1]
    dir_index = lax.axis_index("dir")
    near_index = lax.axis_index("near")
    me = dir_index * nears + near_index
    odd = lax.rem(near_index, 2)
    mate = near_index + 1 - 2 * odd
    half_leaves = half * CHILDREN
    own = pool.at[pl.ds(0, leaf_slots)]
    borrowed = pool.at[pl.ds(leaf_slots, half_leaves)]

    def deltas(index, count):
        steps, bit = [], 1
        while bit < count:
            steps.append((bit, bit - 2 * bit * lax.rem(index // bit, 2)))
            bit *= 2
        return steps

    dir_deltas, near_deltas = deltas(dir_index, dirs), deltas(near_index, nears)

    def partner(step):
        d, n = dir_index, near_index
        for bit, delta in dir_deltas:
            if step // nears & bit:
                d = d + delta
        for bit, delta in near_deltas:
            if step % nears & bit:
                n = n + delta
        return d, n

    load_own = pltpu.make_async_copy(currents, own, load_sem.at[0])
    load_source = pltpu.make_async_copy(near_source_hbm, near_source, small_sem.at[1])
    load_mid = pltpu.make_async_copy(currents, window.at[pl.ds(leaf_slots, leaf_slots)], load_sem.at[2])
    load_tra = pltpu.make_async_copy(translations, tra_v, load_sem.at[3])
    load_rec = pltpu.make_async_copy(receive, rec_v, load_sem.at[4])
    load_near = pltpu.make_async_copy(near_blocks, near_v, load_sem.at[5])

    def start_pieces(source, target, sem, count):
        size = target.shape[0] // count
        for piece in range(count):
            cut = pl.ds(piece * size, size)
            pltpu.make_async_copy(source.at[cut], target.at[cut], sem).start()

    tile_devices = devices // tiles
    tile_dirs = tile_devices // nears
    rows = tile_devices * per
    my_tile = dir_index // tile_dirs

    def load_rows(step):
        tile = flipped(my_tile, tiles - 1 - step, tiles)
        cut = pl.ds(pl.multiple_of(tile * rows, 16), rows)
        return pltpu.make_async_copy(aggregate.at[:, cut, :], agg_v.at[:, cut, :], agg_sem.at[step])

    load_counts = pltpu.make_async_copy(counts_hbm, counts, small_sem.at[0])
    load_counts.start()
    load_own.start()
    for step in range(tiles):
        load_rows(step).start()
    load_tra.start()
    start_pieces(receive, rec_v, load_sem.at[4], 8)
    load_source.start()
    load_mid.start()
    start_pieces(near_blocks, near_v, load_sem.at[5], 8)

    barrier = pltpu.get_barrier_semaphore()
    @pl.when(odd == 0)
    def _():
        pl.semaphore_signal(barrier, inc=1, device_id=(dir_index, mate), device_id_type=MESH)

    @pl.when(odd == 1)
    def _():
        pl.semaphore_wait(barrier, 1)
        pl.semaphore_signal(met_sem, inc=1, device_id=(dir_index, mate), device_id_type=MESH)

    @pl.when(odd == 0)
    def _():
        pl.semaphore_wait(met_sem, 1)

    to_mate = pltpu.make_async_remote_copy(
        src_ref=currents.at[pl.ds((1 - odd) * half_leaves, half_leaves)],
        dst_ref=borrowed,
        send_sem=pair_sem.at[0],
        recv_sem=pair_sem.at[1],
        device_id=(dir_index, mate),
        device_id_type=MESH,
    )
    to_mate.start()

    @pl.when(odd == 0)
    def _():
        for step in range(devices - 2, 0, -2):
            pl.semaphore_signal(barrier, inc=1, device_id=partner(step), device_id_type=MESH)

    load_counts.wait()
    own_count = counts[me]
    mate_count = counts[dir_index * nears + mate]
    even_count = jnp.where(odd == 0, own_count, mate_count)
    load_own.wait()
    to_mate.wait_recv()
    for w in range(half):
        is_own = jnp.where(odd == 0, w < own_count, half + w >= even_count)
        own_slot = jnp.clip(jnp.where(odd == 0, w, half + w - even_count), 0, parent_slots - 1)
        mate_slot = jnp.clip(jnp.where(odd == 0, w - own_count, w), 0, half - 1)
        slot = jnp.where(is_own, own_slot, parent_slots + mate_slot)
        for c in range(CHILDREN):
            values = pool[slot * CHILDREN + c]
            lanes = pl.ds(w * channels, channels)
            stack[pl.ds(2 * c * unknowns, unknowns), lanes] = values
            stack[pl.ds((2 * c + 1) * unknowns, unknowns), lanes] = turned(values.astype(F32)).astype(BF16)

    def hop(buffer, target, index, to, phase, p):
        return pltpu.make_async_remote_copy(
            src_ref=buffer.at[index],
            dst_ref=target.at[me],
            send_sem=a2a_sem.at[phase, p, 0],
            recv_sem=a2a_sem.at[phase, p, 1],
            device_id=to,
            device_id_type=MESH,
        )

    def all_moved(buffer, phase, p, which):
        some = buffer.at[pl.ds(0, devices - 1)]
        pltpu.make_async_copy(some, some, a2a_sem.at[phase, p, which]).wait()

    def radiate(tile):
        start = pl.multiple_of(tile * rows, 16)
        left = jnp.concatenate([agg_v[c, pl.ds(start, rows), :] for c in range(CHILDREN)], axis=1)
        result = jnp.dot(left, stack[...], preferred_element_type=F32)
        for s in range(slots):
            tile_rows[s] = result[:, s * channels : (s + 1) * channels]

    def pack(tile, p):
        first, size, padded = chunks[p]
        for q in range(tile_devices):
            for s in range(slots):
                packs[p][pl.ds((q * slots + s) * padded, size), :] = tile_rows[s, pl.ds(q * per + first, size), :]
        shape = (tile_devices,) + send1[p].shape[1:]
        send1[p][pl.ds(tile * tile_devices, tile_devices)] = packs[p][...].reshape(shape).astype(BF16)

    def all_here():
        @pl.when(odd == 0)
        def _():
            pl.semaphore_wait(barrier, devices // 2 - 1)
            pl.semaphore_signal(met_sem, inc=1, device_id=(dir_index, mate), device_id_type=MESH)

        @pl.when(odd == 1)
        def _():
            pl.semaphore_wait(met_sem, 1)

    def halo(side, block, first=0, size=None):
        size = leaf_slots if size is None else size
        return pltpu.make_async_remote_copy(
            src_ref=currents.at[pl.ds(first, size)],
            dst_ref=window.at[pl.ds(block * leaf_slots + first, size)],
            send_sem=halo_sem.at[0, block // 2],
            recv_sem=halo_sem.at[1, block // 2],
            device_id=(dir_index, near_index + side),
            device_id_type=MESH,
        )

    def start_halo(part):
        first, size = halo_parts[part]
        if size == 0:
            return

        @pl.when(near_index < nears - 1)
        def _():
            halo(1, 0, first, size).start()

        @pl.when(near_index > 0)
        def _():
            halo(-1, 2, first, size).start()

    def radiate_and_send(step, carry):
        tile = flipped(my_tile, tiles - 1 - step, tiles)
        load_rows(step).wait()
        radiate(tile)
        pack(tile, 0)

        @pl.when(step == 0)
        def _():
            all_here()
            start_halo(0)

        for q in range(tile_devices):
            d, n = partner(q)
            d = d + (tile - my_tile) * tile_dirs
            hop(send1[0], recv1[0], d * nears + n, (d, n), 0, 0).start()
        for p in range(1, pieces):
            pack(tile, p)
        return carry

    lax.fori_loop(0, tiles - 1, radiate_and_send, 0)
    load_rows(tiles - 1).wait()
    radiate(my_tile)
    pack(my_tile, 0)
    if tiles == 1:
        all_here()
        start_halo(0)
    for q in range(1, tile_devices):
        d, n = partner(q)
        hop(send1[0], recv1[0], d * nears + n, (d, n), 0, 0).start()
    for p in range(1, pieces):
        pack(my_tile, p)
        start_halo(p)
        for step in range(devices - 1, 0, -1):
            d, n = partner(step)
            hop(send1[p], recv1[p], d * nears + n, (d, n), 0, p).start()

    start_halo(pieces)

    for p in range(pieces):
        recv1[p][me] = send1[p][me]
    joined[...] = jnp.zeros_like(joined)

    load_rec.wait()
    last_first, last_size, _ = chunks[-1]
    last_total = devices * last_size
    for o in range(last_total // 128):
        ends = [(i // last_size) * per + last_first + i % last_size for i in (o * 128, o * 128 + 127)]
        low, high = ends[0] // 128 * 128, (ends[1] // 128 + 1) * 128
        row = lax.broadcasted_iota(jnp.int32, (high - low, 128), 0) + low
        column = lax.broadcasted_iota(jnp.int32, (high - low, 128), 1) + o * 128
        owner = (row * (2**16 // per + 1)) >> 16
        place = row - owner * per - last_first
        chosen = (place >= 0) & (place < last_size) & (owner * last_size + place == column)
        chooser = jnp.where(chosen, 1.0, 0.0).astype(BF16)
        for part in range(2):
            left = rec_v[:, :, pl.ds(part * directions + low, high - low)].reshape(CHILDREN * unknowns, high - low)
            picked = jnp.dot(left, chooser, preferred_element_type=F32).astype(BF16)
            rec_last[:, pl.ds(part * last_total + o * 128, 128)] = picked

    load_tra.wait()
    blocks, listed, _, block_size, doubled = tra_v.shape
    per_block = devices // blocks
    for p in range(pieces):
        first, size, padded = chunks[p]
        message = send1[p].shape[1:]
        all_moved(recv1[p], 0, p, 1)
        for b in range(blocks):
            got = recv1[p][pl.ds(b * per_block, per_block)].astype(F32)
            gathered[p][b] = got.reshape(gathered[p].shape[1:])
        for k in range(size):
            for b in range(blocks):
                summed = None
                for l in range(listed):
                    source = source_blocks[b, l] if listing else 0
                    rows_k = gathered[p][source, pl.ds(k, block_size, stride=padded), :]
                    both = jnp.concatenate([rows_k, turned(rows_k)], axis=0).astype(BF16)
                    part = jnp.dot(tra_v[b, l, first + k], both, preferred_element_type=F32)
                    summed = part if summed is None else summed + part
                incoming[p][b, pl.ds(k, block_size, stride=padded), :] = summed
        for b in range(blocks):
            packed = incoming[p][b].reshape((per_block,) + message)
            send2[p][pl.ds(b * per_block, per_block)] = packed.astype(BF16)
        for step in range(devices - 1, 0, -1):
            d, n = partner(step)
            hop(send2[p], recv2[p], d * nears + n, (d, n), 1, p).start()
        recv2[p][me] = send2[p][me]

    load_mid.wait()
    load_near.wait()
    load_source.wait()

    @pl.when(near_index > 0)
    def _():
        halo(1, 0).wait_recv()

    @pl.when(near_index < nears - 1)
    def _():
        halo(-1, 2).wait_recv()

    base = (me - 1) * leaf_slots
    together = 4 if leaf_slots % 4 == 0 else 1

    def nearby(step, carry):
        for u in range(together):
            i = step * together + u
            rows_at = [near_source[e, i] - base for e in range(near_per)]
            sources = [window[jnp.clip(r, 0, 3 * leaf_slots - 1)] for r in rows_at]
            parts = [near_v[i, e] for e in range(near_per)]
            real = jnp.concatenate([p[:, :unknowns] for p in parts], axis=1)
            imag = jnp.concatenate([p[:, unknowns:] for p in parts], axis=1)
            result = jnp.dot(
                jnp.concatenate([real, imag], axis=0),
                jnp.concatenate(sources, axis=0),
                preferred_element_type=F32,
            )
            near_acc[i] = result[:unknowns] + turned(result[unknowns:])
        return carry

    lax.fori_loop(0, leaf_slots // together, nearby, 0)

    for p in range(pieces - 1):
        first, size, padded = chunks[p]
        all_moved(recv2[p], 1, p, 1)
        spread[p][...] = recv2[p][...].astype(F32).reshape(spread[p].shape)
        for d in range(devices):
            for s in range(slots):
                joined[s, pl.ds(d * per + first, size), :] = spread[p][pl.ds((d * slots + s) * padded, size), :]

    def fill(target, source, total):
        for s in range(slots):
            lanes = pl.ds(s * channels, channels)
            values = source[s]
            target[pl.ds(0, total), lanes] = values.astype(BF16)
            target[pl.ds(total, total), lanes] = turned(values).astype(BF16)

    group = 2

    if pieces > 1:
        fill(fields, joined, directions)

        def absorb_most(step, carry):
            left = rec_v[pl.ds(step * group, group)].reshape(group * unknowns, 2 * directions)
            start = pl.multiple_of(step * group * unknowns, group * unknowns)
            far_acc[pl.ds(start, group * unknowns), :] = jnp.dot(left, fields[...], preferred_element_type=F32)
            return carry

        lax.fori_loop(0, CHILDREN // group, absorb_most, 0)
    else:
        far_acc[...] = jnp.zeros_like(far_acc)

    p = pieces - 1
    first, size, padded = chunks[p]
    all_moved(recv2[p], 1, p, 1)
    spread[p][...] = recv2[p][...].astype(F32).reshape(spread[p].shape)
    for d in range(devices):
        for s in range(slots):
            joined[s, pl.ds(d * size, size), :] = spread[p][pl.ds((d * slots + s) * padded, size), :]
    fill(fields_last, joined.at[:, pl.ds(0, last_total)], last_total)

    def far_copy(c):
        return pltpu.make_async_remote_copy(
            src_ref=far_send.at[c],
            dst_ref=far_recv.at[c],
            send_sem=far_sem.at[0, c],
            recv_sem=far_sem.at[1, c],
            device_id=(dir_index, mate),
            device_id_type=MESH,
        )

    def absorb(step, carry):
        start = pl.multiple_of(step * group * unknowns, group * unknowns)
        far = far_acc[pl.ds(start, group * unknowns), :] + jnp.dot(
            rec_last[pl.ds(start, group * unknowns), :], fields_last[...], preferred_element_type=F32
        )
        for u in range(group):
            c = step * group + u
            for s in range(slots):
                piece = far[u * unknowns : (u + 1) * unknowns, s * channels : (s + 1) * channels]
                far_own[c, s] = piece
                far_send[c, s] = piece.astype(BF16)
            far_copy(c).start()
        return carry

    lax.fori_loop(0, CHILDREN // group, absorb, 0)

    def finish(c, carry):
        far_copy(c).wait_recv()
        for s in range(parent_slots):
            place = jnp.where(odd == 0, s, even_count + s)
            mine_at = place - half * odd
            mine = (mine_at >= 0) & (mine_at < half)
            own_at = jnp.clip(mine_at, 0, half - 1)
            mate_at = jnp.clip(place - half * (1 - odd), 0, half - 1)
            theirs = far_recv[c, 0]
            for w in range(1, half):
                theirs = jnp.where(mate_at == w, far_recv[c, w], theirs)
            far = jnp.where(mine, far_own[c, own_at], theirs.astype(F32))
            total = far + near_acc[s * CHILDREN + c]
            out[s * CHILDREN + c] = jnp.where(s < own_count, total, 0.0).astype(BF16)
        return carry

    lax.fori_loop(0, CHILDREN, finish, 0)

    to_mate.wait_send()
    for p in range(pieces):
        all_moved(send1[p], 0, p, 0)
        all_moved(send2[p], 1, p, 0)
    for c in range(CHILDREN):
        far_copy(c).wait_send()

    @pl.when(near_index < nears - 1)
    def _():
        halo(1, 0).wait_send()

    @pl.when(near_index > 0)
    def _():
        halo(-1, 2).wait_send()


def body(
    currents, counts, near_source, near_blocks, aggregate, receive, translations, source_blocks
):
    dirs, nears = lax.axis_size("dir"), lax.axis_size("near")
    devices = dirs * nears
    leaf_slots, unknowns, channels = currents.shape
    parent_slots = leaf_slots // CHILDREN
    slots = parent_slots // 2
    blocks, listed, per, block_size, doubled = translations.shape
    directions = aggregate.shape[1]
    chunks = chunks_of(per, slots)
    tiles = 4 if dirs % 4 == 0 and directions % 64 == 0 else 1
    tile_devices = devices // tiles
    lanes = slots * channels
    last_total = devices * chunks[-1][1]
    listing = [source_blocks] if blocks > 1 else []
    hbm_spec = pl.BlockSpec(memory_space=pltpu.HBM)
    messages = [(devices, slots * padded // 8, 8, channels) for _, _, padded in chunks]
    exchange = [pltpu.VMEM(m, BF16) for m in messages]
    boxes = [pltpu.VMEM((blocks, block_size * padded, channels), F32) for _, _, padded in chunks]
    scratch = [
        pltpu.VMEM((leaf_slots + slots * CHILDREN, unknowns, channels), BF16),
        pltpu.VMEM((3 * leaf_slots, unknowns, channels), BF16),
        pltpu.VMEM(near_blocks.shape, BF16),
        pltpu.VMEM(aggregate.shape, BF16),
        pltpu.VMEM(receive.shape, BF16),
        pltpu.VMEM(translations.shape, BF16),
        pltpu.VMEM((2 * CHILDREN * unknowns, lanes), BF16),
        pltpu.VMEM((slots, tile_devices * per, channels), F32),
        pltpu.VMEM((slots, directions, channels), F32),
        pltpu.VMEM((2 * directions, lanes), BF16),
        pltpu.VMEM((CHILDREN * unknowns, 2 * last_total), BF16),
        pltpu.VMEM((2 * last_total, lanes), BF16),
        pltpu.VMEM((CHILDREN * unknowns, lanes), F32),
        pltpu.VMEM((CHILDREN, slots, unknowns, channels), F32),
        pltpu.VMEM((CHILDREN, slots, unknowns, channels), BF16),
        pltpu.VMEM((CHILDREN, slots, unknowns, channels), BF16),
        pltpu.VMEM((leaf_slots, unknowns, channels), F32),
        pltpu.SemaphoreType.DMA((6,)),
        pltpu.SemaphoreType.DMA((tiles,)),
        pltpu.SemaphoreType.DMA((2,)),
        pltpu.SemaphoreType.DMA((2, 2)),
        pltpu.SemaphoreType.DMA((2, len(chunks), 2)),
        pltpu.SemaphoreType.DMA((2, CHILDREN)),
        pltpu.SemaphoreType.REGULAR,
        pltpu.SMEM((devices,), jnp.int32),
        pltpu.SMEM((near_blocks.shape[1], leaf_slots), jnp.int32),
        pltpu.SemaphoreType.DMA((2,)),
    ]
    scratch += [pltpu.VMEM((tile_devices * slots * padded, channels), F32) for _, _, padded in chunks]
    scratch += exchange + exchange + boxes + boxes + exchange + exchange
    scratch += [pltpu.VMEM((devices * slots * padded, channels), F32) for _, _, padded in chunks]
    return pl.pallas_call(
        functools.partial(kernel, (dirs, nears, per, slots, chunks, halo_parts_of(leaf_slots, len(chunks)), tiles, blocks > 1)),
        out_shape=jax.ShapeDtypeStruct(currents.shape, BF16),
        in_specs=[pl.BlockSpec(memory_space=pltpu.SMEM)] * len(listing) + [hbm_spec] * 7,
        out_specs=pl.BlockSpec(memory_space=pltpu.VMEM),
        scratch_shapes=scratch,
        compiler_params=pltpu.CompilerParams(
            collective_id=0, has_side_effects=True, vmem_limit_bytes=50 * 2**20
        ),
    )(
        *listing,
        *(
            pltpu.with_memory_space_constraint(array, pltpu.HBM)
            for array in (
                counts,
                near_source.T,
                currents,
                near_blocks,
                aggregate,
                receive,
                translations,
            )
        ),
    )


def solution(mesh):
    return jax.shard_map(
        body,
        mesh=mesh,
        in_specs=(
            P(("dir", "near"), None, None),
            P(),
            P(("dir", "near"), None),
            P(("dir", "near"), None, None, None),
            P(),
            P(),
            P(None, None, ("dir", "near"), None, None),
            P(),
        ),
        out_specs=P(("dir", "near"), None, None),
        check_vma=False,
    )
```

```python
import functools

import jax
import jax.numpy as jnp
from jax import lax
from jax.experimental import pallas as pl
from jax.experimental.pallas import tpu as pltpu
from jax.sharding import PartitionSpec as P

MESH = pl.DeviceIdType.MESH
F32 = jnp.float32
BF16 = jnp.bfloat16
CHILDREN = 8


def turned(values):
    width = values.shape[-1]
    rolled = pltpu.roll(values, width // 2, values.ndim - 1)
    lane = lax.broadcasted_iota(jnp.int32, values.shape, values.ndim - 1)
    return jnp.where(lane < width // 2, -rolled, rolled)


def flipped(index, step, count):
    total = 0
    bit = 1
    while bit < count:
        total = total + bit * lax.rem(index // bit + step // bit, 2)
        bit *= 2
    return total


SHARES = (16, 12, 8)
HALO = (8, 16, 8)


def chunks_of(per, slots):
    sizes = [per * share // sum(SHARES) // 4 * 4 for share in SHARES[:-1]]
    sizes = [size for size in sizes if size]
    sizes.append(per - sum(sizes))
    out, first = [], 0
    for size in sizes:
        out.append((first, size, -(-size * slots // 8) * 8 // slots))
        first += size
    return tuple(out)


def halo_parts_of(leaf_slots, pieces):
    sizes = [HALO[i] * leaf_slots // 32 if i < len(HALO) else 0 for i in range(pieces)]
    sizes.append(leaf_slots - sum(sizes))
    return tuple((sum(sizes[:i]), size) for i, size in enumerate(sizes))


def kernel(dims, *refs):
    dirs, nears, per, slots, chunks, halo_parts, tiles, listing = dims
    devices = dirs * nears
    pieces = len(chunks)
    source_blocks, refs = (refs[0], refs[1:]) if listing else (None, refs)
    counts_hbm, near_source_hbm, currents, near_blocks, aggregate, receive, translations, out = refs[:8]
    scratch = refs[8:]
    (
        pool,
        window,
        near_v,
        agg_v,
        rec_v,
        tra_v,
        stack,
        tile_rows,
        joined,
        fields,
        rec_sorted,
        far_acc,
        far_own,
        far_send,
        far_recv,
        near_acc,
        load_sem,
        agg_sem,
        pair_sem,
        halo_sem,
        a2a_sem,
        far_sem,
        met_sem,
        counts,
        near_source,
        small_sem,
    ) = scratch[:26]
    rest = scratch[26:]
    packs, send1, recv1, gathered, incoming, send2, recv2, spread = (
        rest[i * pieces : (i + 1) * pieces] for i in range(8)
    )
    leaf_slots, unknowns, channels = out.shape
    parent_slots = leaf_slots // CHILDREN
    half = parent_slots // 2
    near_per = near_v.shape[1]
    directions = agg_v.shape[1]
    dir_index = lax.axis_index("dir")
    near_index = lax.axis_index("near")
    me = dir_index * nears + near_index
    odd = lax.rem(near_index, 2)
    mate = near_index + 1 - 2 * odd
    half_leaves = half * CHILDREN
    own = pool.at[pl.ds(0, leaf_slots)]
    borrowed = pool.at[pl.ds(leaf_slots, half_leaves)]

    def deltas(index, count):
        steps, bit = [], 1
        while bit < count:
            steps.append((bit, bit - 2 * bit * lax.rem(index // bit, 2)))
            bit *= 2
        return steps

    dir_deltas, near_deltas = deltas(dir_index, dirs), deltas(near_index, nears)

    def partner(step):
        d, n = dir_index, near_index
        for bit, delta in dir_deltas:
            if step // nears & bit:
                d = d + delta
        for bit, delta in near_deltas:
            if step % nears & bit:
                n = n + delta
        return d, n

    load_own = pltpu.make_async_copy(currents, own, load_sem.at[0])
    load_source = pltpu.make_async_copy(near_source_hbm, near_source, small_sem.at[1])
    load_mid = pltpu.make_async_copy(currents, window.at[pl.ds(leaf_slots, leaf_slots)], load_sem.at[2])
    load_tra = pltpu.make_async_copy(translations, tra_v, load_sem.at[3])
    load_rec = pltpu.make_async_copy(receive, rec_v, load_sem.at[4])
    load_near = pltpu.make_async_copy(near_blocks, near_v, load_sem.at[5])

    def start_pieces(source, target, sem, count):
        size = target.shape[0] // count
        for piece in range(count):
            cut = pl.ds(piece * size, size)
            pltpu.make_async_copy(source.at[cut], target.at[cut], sem).start()

    tile_devices = devices // tiles
    tile_dirs = tile_devices // nears
    rows = tile_devices * per
    my_tile = dir_index // tile_dirs

    def load_rows(step):
        tile = flipped(my_tile, tiles - 1 - step, tiles)
        cut = pl.ds(pl.multiple_of(tile * rows, 16), rows)
        return pltpu.make_async_copy(aggregate.at[:, cut, :], agg_v.at[:, cut, :], agg_sem.at[step])

    load_counts = pltpu.make_async_copy(counts_hbm, counts, small_sem.at[0])
    load_counts.start()
    load_own.start()
    for step in range(tiles):
        load_rows(step).start()

    barrier = pltpu.get_barrier_semaphore()
    @pl.when(odd == 0)
    def _():
        pl.semaphore_signal(barrier, inc=1, device_id=(dir_index, mate), device_id_type=MESH)

    @pl.when(odd == 1)
    def _():
        pl.semaphore_wait(barrier, 1)
        pl.semaphore_signal(met_sem, inc=1, device_id=(dir_index, mate), device_id_type=MESH)

    @pl.when(odd == 0)
    def _():
        pl.semaphore_wait(met_sem, 1)

    to_mate = pltpu.make_async_remote_copy(
        src_ref=currents.at[pl.ds((1 - odd) * half_leaves, half_leaves)],
        dst_ref=borrowed,
        send_sem=pair_sem.at[0],
        recv_sem=pair_sem.at[1],
        device_id=(dir_index, mate),
        device_id_type=MESH,
    )
    to_mate.start()

    @pl.when(odd == 0)
    def _():
        for step in range(devices - 2, 0, -2):
            pl.semaphore_signal(barrier, inc=1, device_id=partner(step), device_id_type=MESH)

    load_counts.wait()
    own_count = counts[me]
    mate_count = counts[dir_index * nears + mate]
    even_count = jnp.where(odd == 0, own_count, mate_count)
    load_own.wait()
    to_mate.wait_recv()
    for w in range(half):
        is_own = jnp.where(odd == 0, w < own_count, half + w >= even_count)
        own_slot = jnp.clip(jnp.where(odd == 0, w, half + w - even_count), 0, parent_slots - 1)
        mate_slot = jnp.clip(jnp.where(odd == 0, w - own_count, w), 0, half - 1)
        slot = jnp.where(is_own, own_slot, parent_slots + mate_slot)
        for c in range(CHILDREN):
            values = pool[slot * CHILDREN + c]
            lanes = pl.ds(w * channels, channels)
            stack[pl.ds(2 * c * unknowns, unknowns), lanes] = values
            stack[pl.ds((2 * c + 1) * unknowns, unknowns), lanes] = turned(values.astype(F32)).astype(BF16)

    def hop(buffer, target, index, to, phase, p):
        return pltpu.make_async_remote_copy(
            src_ref=buffer.at[index],
            dst_ref=target.at[me],
            send_sem=a2a_sem.at[phase, p, 0],
            recv_sem=a2a_sem.at[phase, p, 1],
            device_id=to,
            device_id_type=MESH,
        )

    def all_moved(buffer, phase, p, which):
        some = buffer.at[pl.ds(0, devices - 1)]
        pltpu.make_async_copy(some, some, a2a_sem.at[phase, p, which]).wait()

    def radiate(tile):
        start = pl.multiple_of(tile * rows, 16)
        left = jnp.concatenate([agg_v[c, pl.ds(start, rows), :] for c in range(CHILDREN)], axis=1)
        result = jnp.dot(left, stack[...], preferred_element_type=F32)
        for s in range(slots):
            tile_rows[s] = result[:, s * channels : (s + 1) * channels]

    def pack(tile, p):
        first, size, padded = chunks[p]
        for q in range(tile_devices):
            for s in range(slots):
                packs[p][pl.ds((q * slots + s) * padded, size), :] = tile_rows[s, pl.ds(q * per + first, size), :]
        shape = (tile_devices,) + send1[p].shape[1:]
        send1[p][pl.ds(tile * tile_devices, tile_devices)] = packs[p][...].reshape(shape).astype(BF16)

    def all_here():
        @pl.when(odd == 0)
        def _():
            pl.semaphore_wait(barrier, devices // 2 - 1)
            pl.semaphore_signal(met_sem, inc=1, device_id=(dir_index, mate), device_id_type=MESH)

        @pl.when(odd == 1)
        def _():
            pl.semaphore_wait(met_sem, 1)

    def halo(side, block, first=0, size=None):
        size = leaf_slots if size is None else size
        return pltpu.make_async_remote_copy(
            src_ref=currents.at[pl.ds(first, size)],
            dst_ref=window.at[pl.ds(block * leaf_slots + first, size)],
            send_sem=halo_sem.at[0, block // 2],
            recv_sem=halo_sem.at[1, block // 2],
            device_id=(dir_index, near_index + side),
            device_id_type=MESH,
        )

    def start_halo(part):
        first, size = halo_parts[part]
        if size == 0:
            return

        @pl.when(near_index < nears - 1)
        def _():
            halo(1, 0, first, size).start()

        @pl.when(near_index > 0)
        def _():
            halo(-1, 2, first, size).start()

    def radiate_and_send(step, carry):
        tile = flipped(my_tile, tiles - 1 - step, tiles)
        load_rows(step).wait()
        radiate(tile)
        pack(tile, 0)

        @pl.when(step == 0)
        def _():
            all_here()
            start_halo(0)

        for q in range(tile_devices):
            d, n = partner(q)
            d = d + (tile - my_tile) * tile_dirs
            hop(send1[0], recv1[0], d * nears + n, (d, n), 0, 0).start()
        for p in range(1, pieces):
            pack(tile, p)
        return carry

    lax.fori_loop(0, tiles - 1, radiate_and_send, 0)
    load_rows(tiles - 1).wait()
    load_tra.start()
    load_source.start()
    start_pieces(receive, rec_v, load_sem.at[4], 8)
    load_mid.start()
    start_pieces(near_blocks, near_v, load_sem.at[5], 8)
    radiate(my_tile)
    pack(my_tile, 0)
    if tiles == 1:
        all_here()
        start_halo(0)
    for q in range(1, tile_devices):
        d, n = partner(q)
        hop(send1[0], recv1[0], d * nears + n, (d, n), 0, 0).start()
    for p in range(1, pieces):
        pack(my_tile, p)
        start_halo(p)
        for step in range(devices - 1, 0, -1):
            d, n = partner(step)
            hop(send1[p], recv1[p], d * nears + n, (d, n), 0, p).start()

    start_halo(pieces)

    for p in range(pieces):
        recv1[p][me] = send1[p][me]

    load_rec.wait()
    for first, size, _ in chunks:
        total, place = devices * size, 2 * devices * first
        for o in range(total // 128):
            ends = [(i // size) * per + first + i % size for i in (o * 128, o * 128 + 127)]
            low, high = ends[0] // 128 * 128, (ends[1] // 128 + 1) * 128
            row = lax.broadcasted_iota(jnp.int32, (high - low, 128), 0) + low
            column = lax.broadcasted_iota(jnp.int32, (high - low, 128), 1) + o * 128
            owner = (row * (2**16 // per + 1)) >> 16
            inner = row - owner * per - first
            chosen = (inner >= 0) & (inner < size) & (owner * size + inner == column)
            chooser = jnp.where(chosen, 1.0, 0.0).astype(BF16)
            for part in range(2):
                left = rec_v[:, :, pl.ds(part * directions + low, high - low)].reshape(CHILDREN * unknowns, high - low)
                picked = jnp.dot(left, chooser, preferred_element_type=F32).astype(BF16)
                rec_sorted[:, pl.ds(place + part * total + o * 128, 128)] = picked

    load_tra.wait()
    blocks, listed, _, block_size, doubled = tra_v.shape
    per_block = devices // blocks
    for p in range(pieces):
        first, size, padded = chunks[p]
        message = send1[p].shape[1:]
        all_moved(recv1[p], 0, p, 1)
        for b in range(blocks):
            got = recv1[p][pl.ds(b * per_block, per_block)].astype(F32)
            gathered[p][b] = got.reshape(gathered[p].shape[1:])
        for k in range(size):
            for b in range(blocks):
                summed = None
                for l in range(listed):
                    source = source_blocks[b, l] if listing else 0
                    rows_k = gathered[p][source, pl.ds(k, block_size, stride=padded), :]
                    both = jnp.concatenate([rows_k, turned(rows_k)], axis=0).astype(BF16)
                    part = jnp.dot(tra_v[b, l, first + k], both, preferred_element_type=F32)
                    summed = part if summed is None else summed + part
                incoming[p][b, pl.ds(k, block_size, stride=padded), :] = summed
        for b in range(blocks):
            packed = incoming[p][b].reshape((per_block,) + message)
            send2[p][pl.ds(b * per_block, per_block)] = packed.astype(BF16)
        for step in range(devices - 1, 0, -1):
            d, n = partner(step)
            hop(send2[p], recv2[p], d * nears + n, (d, n), 1, p).start()
        recv2[p][me] = send2[p][me]

    load_mid.wait()
    load_near.wait()
    load_source.wait()

    @pl.when(near_index > 0)
    def _():
        halo(1, 0).wait_recv()

    @pl.when(near_index < nears - 1)
    def _():
        halo(-1, 2).wait_recv()

    base = (me - 1) * leaf_slots
    together = 8 if leaf_slots % 8 == 0 else 1

    def nearby(step, carry):
        for u in range(together):
            i = step * together + u
            rows_at = [near_source[e, i] - base for e in range(near_per)]
            sources = [window[jnp.clip(r, 0, 3 * leaf_slots - 1)] for r in rows_at]
            parts = [near_v[i, e] for e in range(near_per)]
            real = jnp.concatenate([p[:, :unknowns] for p in parts], axis=1)
            imag = jnp.concatenate([p[:, unknowns:] for p in parts], axis=1)
            result = jnp.dot(
                jnp.concatenate([real, imag], axis=0),
                jnp.concatenate(sources, axis=0),
                preferred_element_type=F32,
            )
            near_acc[i] = result[:unknowns] + turned(result[unknowns:])
        return carry

    lax.fori_loop(0, leaf_slots // together, nearby, 0)

    def unpack(p):
        first, size, padded = chunks[p]
        total, place = devices * size, 2 * devices * first
        all_moved(recv2[p], 1, p, 1)
        if size % 8:
            spread[p][...] = recv2[p][...].astype(F32).reshape(spread[p].shape)
        for s in range(slots):
            if size % 8:
                for d in range(devices):
                    joined[pl.ds(d * size, size), :] = spread[p][pl.ds((d * slots + s) * padded, size), :]
                values = joined[pl.ds(0, total), :]
            else:
                values = recv2[p][:, s * size // 8 : (s + 1) * size // 8].astype(F32).reshape(total, channels)
            lanes = pl.ds(s * channels, channels)
            fields[pl.ds(place, total), lanes] = values.astype(BF16)
            fields[pl.ds(place + total, total), lanes] = turned(values).astype(BF16)

    group = 2
    height = group * unknowns
    split = 2 * devices * chunks[-1][0]
    rest_depth = 2 * directions - split

    for p in range(pieces - 1):
        unpack(p)
    if pieces > 1:

        def absorb_most(step, carry):
            start = pl.multiple_of(step * height, height)
            far_acc[pl.ds(start, height), :] = jnp.dot(
                rec_sorted[pl.ds(start, height), pl.ds(0, split)],
                fields[pl.ds(0, split), :],
                preferred_element_type=F32,
            )
            return carry

        lax.fori_loop(0, CHILDREN // group, absorb_most, 0)
    unpack(pieces - 1)

    def far_copy(c):
        return pltpu.make_async_remote_copy(
            src_ref=far_send.at[c],
            dst_ref=far_recv.at[c],
            send_sem=far_sem.at[0, c],
            recv_sem=far_sem.at[1, c],
            device_id=(dir_index, mate),
            device_id_type=MESH,
        )

    def absorb(step, carry):
        start = pl.multiple_of(step * height, height)
        far = jnp.dot(
            rec_sorted[pl.ds(start, height), pl.ds(split, rest_depth)],
            fields[pl.ds(split, rest_depth), :],
            preferred_element_type=F32,
        )
        if pieces > 1:
            far = far + far_acc[pl.ds(start, height), :]
        for u in range(group):
            c = step * group + u
            for s in range(slots):
                piece = far[u * unknowns : (u + 1) * unknowns, s * channels : (s + 1) * channels]
                far_own[c, s] = piece
                far_send[c, s] = piece.astype(BF16)
            far_copy(c).start()
        return carry

    lax.fori_loop(0, CHILDREN // group, absorb, 0)

    def finish(c, carry):
        far_copy(c).wait_recv()
        for s in range(parent_slots):
            place = jnp.where(odd == 0, s, even_count + s)
            mine_at = place - half * odd
            mine = (mine_at >= 0) & (mine_at < half)
            own_at = jnp.clip(mine_at, 0, half - 1)
            mate_at = jnp.clip(place - half * (1 - odd), 0, half - 1)
            theirs = far_recv[c, 0]
            for w in range(1, half):
                theirs = jnp.where(mate_at == w, far_recv[c, w], theirs)
            far = jnp.where(mine, far_own[c, own_at], theirs.astype(F32))
            total = far + near_acc[s * CHILDREN + c]
            out[s * CHILDREN + c] = jnp.where(s < own_count, total, 0.0).astype(BF16)
        return carry

    lax.fori_loop(0, CHILDREN, finish, 0)

    to_mate.wait_send()
    for p in range(pieces):
        all_moved(send1[p], 0, p, 0)
        all_moved(send2[p], 1, p, 0)
    for c in range(CHILDREN):
        far_copy(c).wait_send()

    @pl.when(near_index < nears - 1)
    def _():
        halo(1, 0).wait_send()

    @pl.when(near_index > 0)
    def _():
        halo(-1, 2).wait_send()


def body(
    currents, counts, near_source, near_blocks, aggregate, receive, translations, source_blocks
):
    dirs, nears = lax.axis_size("dir"), lax.axis_size("near")
    devices = dirs * nears
    leaf_slots, unknowns, channels = currents.shape
    parent_slots = leaf_slots // CHILDREN
    slots = parent_slots // 2
    blocks, listed, per, block_size, doubled = translations.shape
    directions = aggregate.shape[1]
    chunks = chunks_of(per, slots)
    tiles = 4 if dirs % 4 == 0 and directions % 64 == 0 else 1
    tile_devices = devices // tiles
    lanes = slots * channels
    listing = [source_blocks] if blocks > 1 else []
    hbm_spec = pl.BlockSpec(memory_space=pltpu.HBM)
    messages = [(devices, slots * padded // 8, 8, channels) for _, _, padded in chunks]
    exchange = [pltpu.VMEM(m, BF16) for m in messages]
    boxes = [pltpu.VMEM((blocks, block_size * padded, channels), F32) for _, _, padded in chunks]
    scratch = [
        pltpu.VMEM((leaf_slots + slots * CHILDREN, unknowns, channels), BF16),
        pltpu.VMEM((3 * leaf_slots, unknowns, channels), BF16),
        pltpu.VMEM(near_blocks.shape, BF16),
        pltpu.VMEM(aggregate.shape, BF16),
        pltpu.VMEM(receive.shape, BF16),
        pltpu.VMEM(translations.shape, BF16),
        pltpu.VMEM((2 * CHILDREN * unknowns, lanes), BF16),
        pltpu.VMEM((slots, tile_devices * per, channels), F32),
        pltpu.VMEM((devices * max(size for _, size, _ in chunks), channels), F32),
        pltpu.VMEM((2 * directions, lanes), BF16),
        pltpu.VMEM((CHILDREN * unknowns, 2 * directions), BF16),
        pltpu.VMEM((CHILDREN * unknowns, lanes), F32),
        pltpu.VMEM((CHILDREN, slots, unknowns, channels), F32),
        pltpu.VMEM((CHILDREN, slots, unknowns, channels), BF16),
        pltpu.VMEM((CHILDREN, slots, unknowns, channels), BF16),
        pltpu.VMEM((leaf_slots, unknowns, channels), F32),
        pltpu.SemaphoreType.DMA((6,)),
        pltpu.SemaphoreType.DMA((tiles,)),
        pltpu.SemaphoreType.DMA((2,)),
        pltpu.SemaphoreType.DMA((2, 2)),
        pltpu.SemaphoreType.DMA((2, len(chunks), 2)),
        pltpu.SemaphoreType.DMA((2, CHILDREN)),
        pltpu.SemaphoreType.REGULAR,
        pltpu.SMEM((devices,), jnp.int32),
        pltpu.SMEM((near_blocks.shape[1], leaf_slots), jnp.int32),
        pltpu.SemaphoreType.DMA((2,)),
    ]
    scratch += [pltpu.VMEM((tile_devices * slots * padded, channels), F32) for _, _, padded in chunks]
    scratch += exchange + exchange + boxes + boxes + exchange + exchange
    scratch += [pltpu.VMEM((devices * slots * padded, channels), F32) for _, _, padded in chunks]
    return pl.pallas_call(
        functools.partial(kernel, (dirs, nears, per, slots, chunks, halo_parts_of(leaf_slots, len(chunks)), tiles, blocks > 1)),
        out_shape=jax.ShapeDtypeStruct(currents.shape, BF16),
        in_specs=[pl.BlockSpec(memory_space=pltpu.SMEM)] * len(listing) + [hbm_spec] * 7,
        out_specs=pl.BlockSpec(memory_space=pltpu.VMEM),
        scratch_shapes=scratch,
        compiler_params=pltpu.CompilerParams(
            collective_id=0, has_side_effects=True, vmem_limit_bytes=50 * 2**20
        ),
    )(
        *listing,
        *(
            pltpu.with_memory_space_constraint(array, pltpu.HBM)
            for array in (
                counts,
                near_source.T,
                currents,
                near_blocks,
                aggregate,
                receive,
                translations,
            )
        ),
    )


def solution(mesh):
    return jax.shard_map(
        body,
        mesh=mesh,
        in_specs=(
            P(("dir", "near"), None, None),
            P(),
            P(("dir", "near"), None),
            P(("dir", "near"), None, None, None),
            P(),
            P(),
            P(None, None, ("dir", "near"), None, None),
            P(),
        ),
        out_specs=P(("dir", "near"), None, None),
        check_vma=False,
    )
```

```python
import functools

import jax
import jax.numpy as jnp
from jax import lax
from jax.experimental import pallas as pl
from jax.experimental.pallas import tpu as pltpu
from jax.sharding import PartitionSpec as P

MESH = pl.DeviceIdType.MESH
F32 = jnp.float32
BF16 = jnp.bfloat16
CHILDREN = 8


def turned(values):
    width = values.shape[-1]
    rolled = pltpu.roll(values, width // 2, values.ndim - 1)
    lane = lax.broadcasted_iota(jnp.int32, values.shape, values.ndim - 1)
    return jnp.where(lane < width // 2, -rolled, rolled)


def flipped(index, step, count):
    total = 0
    bit = 1
    while bit < count:
        total = total + bit * lax.rem(index // bit + step // bit, 2)
        bit *= 2
    return total


SHARES = (12, 12, 12)
HALO = (8, 16, 8)


def chunks_of(per, slots):
    sizes = [per * share // sum(SHARES) // 4 * 4 for share in SHARES[:-1]]
    sizes = [size for size in sizes if size]
    sizes.append(per - sum(sizes))
    out, first = [], 0
    for size in sizes:
        out.append((first, size, -(-size * slots // 8) * 8 // slots))
        first += size
    return tuple(out)


def halo_parts_of(leaf_slots, pieces):
    sizes = [HALO[i] * leaf_slots // 32 if i < len(HALO) else 0 for i in range(pieces)]
    sizes.append(leaf_slots - sum(sizes))
    return tuple((sum(sizes[:i]), size) for i, size in enumerate(sizes))


def kernel(dims, *refs):
    dirs, nears, per, slots, chunks, halo_parts, tiles, listing = dims
    devices = dirs * nears
    pieces = len(chunks)
    source_blocks, refs = (refs[0], refs[1:]) if listing else (None, refs)
    counts_hbm, near_source_hbm, currents, near_blocks, aggregate, receive, translations, out = refs[:8]
    scratch = refs[8:]
    (
        pool,
        window,
        near_v,
        agg_v,
        rec_v,
        tra_v,
        stack,
        tile_rows,
        joined,
        fields,
        rec_sorted,
        far_acc,
        far_own,
        far_send,
        far_recv,
        near_acc,
        load_sem,
        agg_sem,
        pair_sem,
        halo_sem,
        a2a_sem,
        far_sem,
        met_sem,
        counts,
        near_source,
        small_sem,
    ) = scratch[:26]
    rest = scratch[26:]
    packs, send1, recv1, gathered, incoming, send2, recv2, spread = (
        rest[i * pieces : (i + 1) * pieces] for i in range(8)
    )
    leaf_slots, unknowns, channels = out.shape
    parent_slots = leaf_slots // CHILDREN
    half = parent_slots // 2
    near_per = near_v.shape[1]
    directions = agg_v.shape[1]
    dir_index = lax.axis_index("dir")
    near_index = lax.axis_index("near")
    me = dir_index * nears + near_index
    odd = lax.rem(near_index, 2)
    mate = near_index + 1 - 2 * odd
    half_leaves = half * CHILDREN
    own = pool.at[pl.ds(0, leaf_slots)]
    borrowed = pool.at[pl.ds(leaf_slots, half_leaves)]

    def deltas(index, count):
        steps, bit = [], 1
        while bit < count:
            steps.append((bit, bit - 2 * bit * lax.rem(index // bit, 2)))
            bit *= 2
        return steps

    dir_deltas, near_deltas = deltas(dir_index, dirs), deltas(near_index, nears)

    def partner(step):
        d, n = dir_index, near_index
        for bit, delta in dir_deltas:
            if step // nears & bit:
                d = d + delta
        for bit, delta in near_deltas:
            if step % nears & bit:
                n = n + delta
        return d, n

    barrier = pltpu.get_barrier_semaphore()

    @pl.when(odd == 0)
    def _():
        pl.semaphore_signal(barrier, inc=1, device_id=(dir_index, mate), device_id_type=MESH)

    load_own = pltpu.make_async_copy(currents, own, load_sem.at[0])
    load_source = pltpu.make_async_copy(near_source_hbm, near_source, small_sem.at[1])
    load_mid = pltpu.make_async_copy(currents, window.at[pl.ds(leaf_slots, leaf_slots)], load_sem.at[2])
    load_tra = pltpu.make_async_copy(translations, tra_v, load_sem.at[3])
    load_rec = pltpu.make_async_copy(receive, rec_v, load_sem.at[4])
    load_near = pltpu.make_async_copy(near_blocks, near_v, load_sem.at[5])

    def start_pieces(source, target, sem, count):
        size = target.shape[0] // count
        for piece in range(count):
            cut = pl.ds(piece * size, size)
            pltpu.make_async_copy(source.at[cut], target.at[cut], sem).start()

    tile_devices = devices // tiles
    tile_dirs = tile_devices // nears
    rows = tile_devices * per
    my_tile = dir_index // tile_dirs

    def load_rows(step):
        tile = flipped(my_tile, tiles - 1 - step, tiles)
        cut = pl.ds(pl.multiple_of(tile * rows, 16), rows)
        return pltpu.make_async_copy(aggregate.at[:, cut, :], agg_v.at[:, cut, :], agg_sem.at[step])

    load_counts = pltpu.make_async_copy(counts_hbm, counts, small_sem.at[0])
    load_counts.start()
    load_own.start()
    for step in range(tiles):
        load_rows(step).start()

    @pl.when(odd == 1)
    def _():
        pl.semaphore_wait(barrier, 1)
        pl.semaphore_signal(met_sem, inc=1, device_id=(dir_index, mate), device_id_type=MESH)

    @pl.when(odd == 0)
    def _():
        pl.semaphore_wait(met_sem, 1)

    to_mate = pltpu.make_async_remote_copy(
        src_ref=currents.at[pl.ds((1 - odd) * half_leaves, half_leaves)],
        dst_ref=borrowed,
        send_sem=pair_sem.at[0],
        recv_sem=pair_sem.at[1],
        device_id=(dir_index, mate),
        device_id_type=MESH,
    )
    to_mate.start()

    @pl.when(odd == 0)
    def _():
        for step in range(devices - 2, 0, -2):
            pl.semaphore_signal(barrier, inc=1, device_id=partner(step), device_id_type=MESH)

    load_counts.wait()
    own_count = counts[me]
    mate_count = counts[dir_index * nears + mate]
    even_count = jnp.where(odd == 0, own_count, mate_count)
    load_own.wait()
    to_mate.wait_recv()
    for w in range(half):
        is_own = jnp.where(odd == 0, w < own_count, half + w >= even_count)
        own_slot = jnp.clip(jnp.where(odd == 0, w, half + w - even_count), 0, parent_slots - 1)
        mate_slot = jnp.clip(jnp.where(odd == 0, w - own_count, w), 0, half - 1)
        slot = jnp.where(is_own, own_slot, parent_slots + mate_slot)
        for c in range(CHILDREN):
            values = pool[slot * CHILDREN + c]
            lanes = pl.ds(w * channels, channels)
            stack[pl.ds(2 * c * unknowns, unknowns), lanes] = values
            stack[pl.ds((2 * c + 1) * unknowns, unknowns), lanes] = turned(values.astype(F32)).astype(BF16)

    def hop(buffer, target, index, to, phase, p):
        return pltpu.make_async_remote_copy(
            src_ref=buffer.at[index],
            dst_ref=target.at[me],
            send_sem=a2a_sem.at[phase, p, 0],
            recv_sem=a2a_sem.at[phase, p, 1],
            device_id=to,
            device_id_type=MESH,
        )

    def all_moved(buffer, phase, p, which):
        some = buffer.at[pl.ds(0, devices - 1)]
        pltpu.make_async_copy(some, some, a2a_sem.at[phase, p, which]).wait()

    def radiate(tile):
        start = pl.multiple_of(tile * rows, 16)
        left = jnp.concatenate([agg_v[c, pl.ds(start, rows), :] for c in range(CHILDREN)], axis=1)
        result = jnp.dot(left, stack[...], preferred_element_type=F32)
        for s in range(slots):
            tile_rows[s] = result[:, s * channels : (s + 1) * channels]

    def pack(tile, p):
        first, size, padded = chunks[p]
        for q in range(tile_devices):
            for s in range(slots):
                packs[p][pl.ds((q * slots + s) * padded, size), :] = tile_rows[s, pl.ds(q * per + first, size), :]
        shape = (tile_devices,) + send1[p].shape[1:]
        send1[p][pl.ds(tile * tile_devices, tile_devices)] = packs[p][...].reshape(shape).astype(BF16)

    def all_here():
        @pl.when(odd == 0)
        def _():
            pl.semaphore_wait(barrier, devices // 2 - 1)
            pl.semaphore_signal(met_sem, inc=1, device_id=(dir_index, mate), device_id_type=MESH)

        @pl.when(odd == 1)
        def _():
            pl.semaphore_wait(met_sem, 1)

    def halo(side, block, first=0, size=None):
        size = leaf_slots if size is None else size
        return pltpu.make_async_remote_copy(
            src_ref=currents.at[pl.ds(first, size)],
            dst_ref=window.at[pl.ds(block * leaf_slots + first, size)],
            send_sem=halo_sem.at[0, block // 2],
            recv_sem=halo_sem.at[1, block // 2],
            device_id=(dir_index, near_index + side),
            device_id_type=MESH,
        )

    def start_halo(part):
        first, size = halo_parts[part]
        if size == 0:
            return

        @pl.when(near_index < nears - 1)
        def _():
            halo(1, 0, first, size).start()

        @pl.when(near_index > 0)
        def _():
            halo(-1, 2, first, size).start()

    def radiate_and_send(step, carry):
        tile = flipped(my_tile, tiles - 1 - step, tiles)
        load_rows(step).wait()
        radiate(tile)
        pack(tile, 0)

        @pl.when(step == 0)
        def _():
            all_here()
            start_halo(0)

        for q in range(tile_devices):
            d, n = partner(q)
            d = d + (tile - my_tile) * tile_dirs
            hop(send1[0], recv1[0], d * nears + n, (d, n), 0, 0).start()
        for p in range(1, pieces):
            pack(tile, p)
        return carry

    lax.fori_loop(0, tiles - 1, radiate_and_send, 0)
    load_rows(tiles - 1).wait()
    load_tra.start()
    load_source.start()
    start_pieces(receive, rec_v, load_sem.at[4], 8)
    load_mid.start()
    start_pieces(near_blocks, near_v, load_sem.at[5], 8)
    radiate(my_tile)
    pack(my_tile, 0)
    if tiles == 1:
        all_here()
        start_halo(0)
    for q in range(1, tile_devices):
        d, n = partner(q)
        hop(send1[0], recv1[0], d * nears + n, (d, n), 0, 0).start()
    for p in range(1, pieces):
        pack(my_tile, p)
        start_halo(p)
        for step in range(devices - 1, 0, -1):
            d, n = partner(step)
            hop(send1[p], recv1[p], d * nears + n, (d, n), 0, p).start()

    start_halo(pieces)

    for p in range(pieces):
        recv1[p][me] = send1[p][me]

    load_rec.wait()
    for first, size, _ in chunks:
        total, place = devices * size, 2 * devices * first
        for o in range(total // 128):
            ends = [(i // size) * per + first + i % size for i in (o * 128, o * 128 + 127)]
            low, high = ends[0] // 128 * 128, (ends[1] // 128 + 1) * 128
            row = lax.broadcasted_iota(jnp.int32, (high - low, 128), 0) + low
            column = lax.broadcasted_iota(jnp.int32, (high - low, 128), 1) + o * 128
            owner = (row * (2**16 // per + 1)) >> 16
            inner = row - owner * per - first
            chosen = (inner >= 0) & (inner < size) & (owner * size + inner == column)
            chooser = jnp.where(chosen, 1.0, 0.0).astype(BF16)
            for part in range(2):
                left = rec_v[:, :, pl.ds(part * directions + low, high - low)].reshape(CHILDREN * unknowns, high - low)
                picked = jnp.dot(left, chooser, preferred_element_type=F32).astype(BF16)
                rec_sorted[:, pl.ds(place + part * total + o * 128, 128)] = picked

    load_tra.wait()
    blocks, listed, _, block_size, doubled = tra_v.shape
    per_block = devices // blocks
    for p in range(pieces):
        first, size, padded = chunks[p]
        message = send1[p].shape[1:]
        all_moved(recv1[p], 0, p, 1)
        for b in range(blocks):
            got = recv1[p][pl.ds(b * per_block, per_block)].astype(F32)
            gathered[p][b] = got.reshape(gathered[p].shape[1:])
        for k in range(size):
            for b in range(blocks):
                summed = None
                for l in range(listed):
                    source = source_blocks[b, l] if listing else 0
                    rows_k = gathered[p][source, pl.ds(k, block_size, stride=padded), :]
                    both = jnp.concatenate([rows_k, turned(rows_k)], axis=0).astype(BF16)
                    part = jnp.dot(tra_v[b, l, first + k], both, preferred_element_type=F32)
                    summed = part if summed is None else summed + part
                incoming[p][b, pl.ds(k, block_size, stride=padded), :] = summed
        for b in range(blocks):
            packed = incoming[p][b].reshape((per_block,) + message)
            send2[p][pl.ds(b * per_block, per_block)] = packed.astype(BF16)
        for step in range(devices - 1, 0, -1):
            d, n = partner(step)
            hop(send2[p], recv2[p], d * nears + n, (d, n), 1, p).start()
        recv2[p][me] = send2[p][me]

    load_mid.wait()
    load_near.wait()
    load_source.wait()

    @pl.when(near_index > 0)
    def _():
        halo(1, 0).wait_recv()

    @pl.when(near_index < nears - 1)
    def _():
        halo(-1, 2).wait_recv()

    base = (me - 1) * leaf_slots
    together = 8 if leaf_slots % 8 == 0 else 1

    def nearby(step, carry):
        for u in range(together):
            i = step * together + u
            rows_at = [near_source[e, i] - base for e in range(near_per)]
            sources = [window[jnp.clip(r, 0, 3 * leaf_slots - 1)] for r in rows_at]
            parts = [near_v[i, e] for e in range(near_per)]
            real = jnp.concatenate([p[:, :unknowns] for p in parts], axis=1)
            imag = jnp.concatenate([p[:, unknowns:] for p in parts], axis=1)
            result = jnp.dot(
                jnp.concatenate([real, imag], axis=0),
                jnp.concatenate(sources, axis=0),
                preferred_element_type=F32,
            )
            near_acc[i] = result[:unknowns] + turned(result[unknowns:])
        return carry

    lax.fori_loop(0, leaf_slots // together, nearby, 0)

    def unpack(p):
        first, size, padded = chunks[p]
        total, place = devices * size, 2 * devices * first
        all_moved(recv2[p], 1, p, 1)
        if size % 8:
            spread[p][...] = recv2[p][...].astype(F32).reshape(spread[p].shape)
        for s in range(slots):
            if size % 8:
                for d in range(devices):
                    joined[pl.ds(d * size, size), :] = spread[p][pl.ds((d * slots + s) * padded, size), :]
                values = joined[pl.ds(0, total), :]
            else:
                values = recv2[p][:, s * size // 8 : (s + 1) * size // 8].astype(F32).reshape(total, channels)
            lanes = pl.ds(s * channels, channels)
            fields[pl.ds(place, total), lanes] = values.astype(BF16)
            fields[pl.ds(place + total, total), lanes] = turned(values).astype(BF16)

    group = 4
    height = group * unknowns
    split = 2 * devices * chunks[-1][0]
    rest_depth = 2 * directions - split

    for p in range(pieces - 1):
        unpack(p)
    if pieces > 1:

        def absorb_most(step, carry):
            start = pl.multiple_of(step * height, height)
            far_acc[pl.ds(start, height), :] = jnp.dot(
                rec_sorted[pl.ds(start, height), pl.ds(0, split)],
                fields[pl.ds(0, split), :],
                preferred_element_type=F32,
            )
            return carry

        lax.fori_loop(0, CHILDREN // group, absorb_most, 0)
    unpack(pieces - 1)

    def far_copy(c):
        return pltpu.make_async_remote_copy(
            src_ref=far_send.at[c],
            dst_ref=far_recv.at[c],
            send_sem=far_sem.at[0, c],
            recv_sem=far_sem.at[1, c],
            device_id=(dir_index, mate),
            device_id_type=MESH,
        )

    def absorb(step, carry):
        start = pl.multiple_of(step * height, height)
        far = jnp.dot(
            rec_sorted[pl.ds(start, height), pl.ds(split, rest_depth)],
            fields[pl.ds(split, rest_depth), :],
            preferred_element_type=F32,
        )
        if pieces > 1:
            far = far + far_acc[pl.ds(start, height), :]
        for u in range(group):
            c = step * group + u
            for s in range(slots):
                piece = far[u * unknowns : (u + 1) * unknowns, s * channels : (s + 1) * channels]
                far_own[c, s] = piece
                far_send[c, s] = piece.astype(BF16)
            far_copy(c).start()
        return carry

    lax.fori_loop(0, CHILDREN // group, absorb, 0)

    def finish(c, carry):
        far_copy(c).wait_recv()
        for s in range(parent_slots):
            place = jnp.where(odd == 0, s, even_count + s)
            mine_at = place - half * odd
            mine = (mine_at >= 0) & (mine_at < half)
            own_at = jnp.clip(mine_at, 0, half - 1)
            mate_at = jnp.clip(place - half * (1 - odd), 0, half - 1)
            theirs = far_recv[c, 0]
            for w in range(1, half):
                theirs = jnp.where(mate_at == w, far_recv[c, w], theirs)
            far = jnp.where(mine, far_own[c, own_at], theirs.astype(F32))
            total = far + near_acc[s * CHILDREN + c]
            out[s * CHILDREN + c] = jnp.where(s < own_count, total, 0.0).astype(BF16)
        return carry

    lax.fori_loop(0, CHILDREN, finish, 0)

    to_mate.wait_send()
    for p in range(pieces):
        all_moved(send1[p], 0, p, 0)
        all_moved(send2[p], 1, p, 0)
    for c in range(CHILDREN):
        far_copy(c).wait_send()

    @pl.when(near_index < nears - 1)
    def _():
        halo(1, 0).wait_send()

    @pl.when(near_index > 0)
    def _():
        halo(-1, 2).wait_send()


def body(
    currents, counts, near_source, near_blocks, aggregate, receive, translations, source_blocks
):
    dirs, nears = lax.axis_size("dir"), lax.axis_size("near")
    devices = dirs * nears
    leaf_slots, unknowns, channels = currents.shape
    parent_slots = leaf_slots // CHILDREN
    slots = parent_slots // 2
    blocks, listed, per, block_size, doubled = translations.shape
    directions = aggregate.shape[1]
    chunks = chunks_of(per, slots)
    tiles = 4 if dirs % 4 == 0 and directions % 64 == 0 else 1
    tile_devices = devices // tiles
    lanes = slots * channels
    listing = [source_blocks] if blocks > 1 else []
    hbm_spec = pl.BlockSpec(memory_space=pltpu.HBM)
    messages = [(devices, slots * padded // 8, 8, channels) for _, _, padded in chunks]
    exchange = [pltpu.VMEM(m, BF16) for m in messages]
    boxes = [pltpu.VMEM((blocks, block_size * padded, channels), F32) for _, _, padded in chunks]
    scratch = [
        pltpu.VMEM((leaf_slots + slots * CHILDREN, unknowns, channels), BF16),
        pltpu.VMEM((3 * leaf_slots, unknowns, channels), BF16),
        pltpu.VMEM(near_blocks.shape, BF16),
        pltpu.VMEM(aggregate.shape, BF16),
        pltpu.VMEM(receive.shape, BF16),
        pltpu.VMEM(translations.shape, BF16),
        pltpu.VMEM((2 * CHILDREN * unknowns, lanes), BF16),
        pltpu.VMEM((slots, tile_devices * per, channels), F32),
        pltpu.VMEM((devices * max(size for _, size, _ in chunks), channels), F32),
        pltpu.VMEM((2 * directions, lanes), BF16),
        pltpu.VMEM((CHILDREN * unknowns, 2 * directions), BF16),
        pltpu.VMEM((CHILDREN * unknowns, lanes), F32),
        pltpu.VMEM((CHILDREN, slots, unknowns, channels), F32),
        pltpu.VMEM((CHILDREN, slots, unknowns, channels), BF16),
        pltpu.VMEM((CHILDREN, slots, unknowns, channels), BF16),
        pltpu.VMEM((leaf_slots, unknowns, channels), F32),
        pltpu.SemaphoreType.DMA((6,)),
        pltpu.SemaphoreType.DMA((tiles,)),
        pltpu.SemaphoreType.DMA((2,)),
        pltpu.SemaphoreType.DMA((2, 2)),
        pltpu.SemaphoreType.DMA((2, len(chunks), 2)),
        pltpu.SemaphoreType.DMA((2, CHILDREN)),
        pltpu.SemaphoreType.REGULAR,
        pltpu.SMEM((devices,), jnp.int32),
        pltpu.SMEM((near_blocks.shape[1], leaf_slots), jnp.int32),
        pltpu.SemaphoreType.DMA((2,)),
    ]
    scratch += [pltpu.VMEM((tile_devices * slots * padded, channels), F32) for _, _, padded in chunks]
    scratch += exchange + exchange + boxes + boxes + exchange + exchange
    scratch += [pltpu.VMEM((devices * slots * padded, channels), F32) for _, _, padded in chunks]
    return pl.pallas_call(
        functools.partial(kernel, (dirs, nears, per, slots, chunks, halo_parts_of(leaf_slots, len(chunks)), tiles, blocks > 1)),
        out_shape=jax.ShapeDtypeStruct(currents.shape, BF16),
        in_specs=[pl.BlockSpec(memory_space=pltpu.SMEM)] * len(listing) + [hbm_spec] * 7,
        out_specs=pl.BlockSpec(memory_space=pltpu.VMEM),
        scratch_shapes=scratch,
        compiler_params=pltpu.CompilerParams(
            collective_id=0, has_side_effects=True, vmem_limit_bytes=50 * 2**20
        ),
    )(
        *listing,
        *(
            pltpu.with_memory_space_constraint(array, pltpu.HBM)
            for array in (
                counts,
                near_source.T,
                currents,
                near_blocks,
                aggregate,
                receive,
                translations,
            )
        ),
    )


def solution(mesh):
    return jax.shard_map(
        body,
        mesh=mesh,
        in_specs=(
            P(("dir", "near"), None, None),
            P(),
            P(("dir", "near"), None),
            P(("dir", "near"), None, None, None),
            P(),
            P(),
            P(None, None, ("dir", "near"), None, None),
            P(),
        ),
        out_specs=P(("dir", "near"), None, None),
        check_vma=False,
    )
```

```python
import functools

import jax
import jax.numpy as jnp
from jax import lax
from jax.experimental import pallas as pl
from jax.experimental.pallas import tpu as pltpu
from jax.sharding import PartitionSpec as P

MESH = pl.DeviceIdType.MESH
F32 = jnp.float32
BF16 = jnp.bfloat16
CHILDREN = 8


def turned(values):
    width = values.shape[-1]
    rolled = pltpu.roll(values, width // 2, values.ndim - 1)
    lane = lax.broadcasted_iota(jnp.int32, values.shape, values.ndim - 1)
    return jnp.where(lane < width // 2, -rolled, rolled)


def flipped(index, step, count):
    total = 0
    bit = 1
    while bit < count:
        total = total + bit * lax.rem(index // bit + step // bit, 2)
        bit *= 2
    return total


SHARES = (12, 12, 12)
HALO = (8, 14, 8)


def chunks_of(per, slots):
    sizes = [per * share // sum(SHARES) // 4 * 4 for share in SHARES[:-1]]
    sizes = [size for size in sizes if size]
    sizes.append(per - sum(sizes))
    out, first = [], 0
    for size in sizes:
        out.append((first, size, -(-size * slots // 8) * 8 // slots))
        first += size
    return tuple(out)


def halo_parts_of(leaf_slots, pieces):
    sizes = [HALO[i] * leaf_slots // 32 if i < len(HALO) else 0 for i in range(pieces)]
    sizes.append(leaf_slots - sum(sizes))
    return tuple((sum(sizes[:i]), size) for i, size in enumerate(sizes))


def kernel(dims, *refs):
    dirs, nears, per, slots, chunks, halo_parts, tiles, listing = dims
    devices = dirs * nears
    pieces = len(chunks)
    source_blocks, refs = (refs[0], refs[1:]) if listing else (None, refs)
    counts_hbm, near_source_hbm, currents, near_blocks, aggregate, receive, translations, out = refs[:8]
    scratch = refs[8:]
    (
        pool,
        window,
        near_v,
        agg_v,
        rec_v,
        tra_v,
        stack,
        tile_rows,
        joined,
        fields,
        rec_sorted,
        far_acc,
        far_own,
        far_send,
        far_recv,
        near_acc,
        load_sem,
        agg_sem,
        pair_sem,
        halo_sem,
        a2a_sem,
        far_sem,
        met_sem,
        counts,
        near_source,
        small_sem,
    ) = scratch[:26]
    rest = scratch[26:]
    packs, send1, recv1, gathered, incoming, send2, recv2, spread = (
        rest[i * pieces : (i + 1) * pieces] for i in range(8)
    )
    leaf_slots, unknowns, channels = out.shape
    parent_slots = leaf_slots // CHILDREN
    half = parent_slots // 2
    near_per = near_v.shape[1]
    directions = agg_v.shape[1]
    dir_index = lax.axis_index("dir")
    near_index = lax.axis_index("near")
    me = dir_index * nears + near_index
    odd = lax.rem(near_index, 2)
    mate = near_index + 1 - 2 * odd
    half_leaves = half * CHILDREN
    own = pool.at[pl.ds(0, leaf_slots)]
    borrowed = pool.at[pl.ds(leaf_slots, half_leaves)]

    def deltas(index, count):
        steps, bit = [], 1
        while bit < count:
            steps.append((bit, bit - 2 * bit * lax.rem(index // bit, 2)))
            bit *= 2
        return steps

    dir_deltas, near_deltas = deltas(dir_index, dirs), deltas(near_index, nears)

    def partner(step):
        d, n = dir_index, near_index
        for bit, delta in dir_deltas:
            if step // nears & bit:
                d = d + delta
        for bit, delta in near_deltas:
            if step % nears & bit:
                n = n + delta
        return d, n

    barrier = pltpu.get_barrier_semaphore()

    @pl.when(odd == 0)
    def _():
        pl.semaphore_signal(barrier, inc=1, device_id=(dir_index, mate), device_id_type=MESH)

    load_own = pltpu.make_async_copy(currents, own, load_sem.at[0])
    load_source = pltpu.make_async_copy(near_source_hbm, near_source, small_sem.at[1])
    load_mid = pltpu.make_async_copy(currents, window.at[pl.ds(leaf_slots, leaf_slots)], load_sem.at[2])
    load_tra = pltpu.make_async_copy(translations, tra_v, load_sem.at[3])
    load_rec = pltpu.make_async_copy(receive, rec_v, load_sem.at[4])
    load_near = pltpu.make_async_copy(near_blocks, near_v, load_sem.at[5])

    def start_pieces(source, target, sem, count):
        size = target.shape[0] // count
        for piece in range(count):
            cut = pl.ds(piece * size, size)
            pltpu.make_async_copy(source.at[cut], target.at[cut], sem).start()

    tile_devices = devices // tiles
    tile_dirs = tile_devices // nears
    rows = tile_devices * per
    my_tile = dir_index // tile_dirs

    def load_rows(step):
        tile = flipped(my_tile, tiles - 1 - step, tiles)
        cut = pl.ds(pl.multiple_of(tile * rows, 16), rows)
        return pltpu.make_async_copy(aggregate.at[:, cut, :], agg_v.at[:, cut, :], agg_sem.at[step])

    load_counts = pltpu.make_async_copy(counts_hbm, counts, small_sem.at[0])
    load_counts.start()
    load_own.start()
    for step in range(tiles):
        load_rows(step).start()

    @pl.when(odd == 1)
    def _():
        pl.semaphore_wait(barrier, 1)
        pl.semaphore_signal(met_sem, inc=1, device_id=(dir_index, mate), device_id_type=MESH)

    @pl.when(odd == 0)
    def _():
        pl.semaphore_wait(met_sem, 1)

    to_mate = pltpu.make_async_remote_copy(
        src_ref=currents.at[pl.ds((1 - odd) * half_leaves, half_leaves)],
        dst_ref=borrowed,
        send_sem=pair_sem.at[0],
        recv_sem=pair_sem.at[1],
        device_id=(dir_index, mate),
        device_id_type=MESH,
    )
    to_mate.start()

    @pl.when(odd == 0)
    def _():
        for step in range(devices - 2, 0, -2):
            pl.semaphore_signal(barrier, inc=1, device_id=partner(step), device_id_type=MESH)

    load_counts.wait()
    own_count = counts[me]
    mate_count = counts[dir_index * nears + mate]
    even_count = jnp.where(odd == 0, own_count, mate_count)
    load_own.wait()
    to_mate.wait_recv()
    for w in range(half):
        is_own = jnp.where(odd == 0, w < own_count, half + w >= even_count)
        own_slot = jnp.clip(jnp.where(odd == 0, w, half + w - even_count), 0, parent_slots - 1)
        mate_slot = jnp.clip(jnp.where(odd == 0, w - own_count, w), 0, half - 1)
        slot = jnp.where(is_own, own_slot, parent_slots + mate_slot)
        for c in range(CHILDREN):
            values = pool[slot * CHILDREN + c]
            lanes = pl.ds(w * channels, channels)
            stack[pl.ds(2 * c * unknowns, unknowns), lanes] = values
            stack[pl.ds((2 * c + 1) * unknowns, unknowns), lanes] = turned(values.astype(F32)).astype(BF16)

    def hop(buffer, target, index, to, phase, p):
        return pltpu.make_async_remote_copy(
            src_ref=buffer.at[index],
            dst_ref=target.at[me],
            send_sem=a2a_sem.at[phase, p, 0],
            recv_sem=a2a_sem.at[phase, p, 1],
            device_id=to,
            device_id_type=MESH,
        )

    def all_moved(buffer, phase, p, which):
        some = buffer.at[pl.ds(0, devices - 1)]
        pltpu.make_async_copy(some, some, a2a_sem.at[phase, p, which]).wait()

    def radiate(tile):
        start = pl.multiple_of(tile * rows, 16)
        left = jnp.concatenate([agg_v[c, pl.ds(start, rows), :] for c in range(CHILDREN)], axis=1)
        result = jnp.dot(left, stack[...], preferred_element_type=F32)
        for s in range(slots):
            tile_rows[s] = result[:, s * channels : (s + 1) * channels]

    def pack(tile, p):
        first, size, padded = chunks[p]
        for q in range(tile_devices):
            for s in range(slots):
                packs[p][pl.ds((q * slots + s) * padded, size), :] = tile_rows[s, pl.ds(q * per + first, size), :]
        shape = (tile_devices,) + send1[p].shape[1:]
        send1[p][pl.ds(tile * tile_devices, tile_devices)] = packs[p][...].reshape(shape).astype(BF16)

    def all_here():
        @pl.when(odd == 0)
        def _():
            pl.semaphore_wait(barrier, devices // 2 - 1)
            pl.semaphore_signal(met_sem, inc=1, device_id=(dir_index, mate), device_id_type=MESH)

        @pl.when(odd == 1)
        def _():
            pl.semaphore_wait(met_sem, 1)

    def halo(side, block, first=0, size=None):
        size = leaf_slots if size is None else size
        return pltpu.make_async_remote_copy(
            src_ref=currents.at[pl.ds(first, size)],
            dst_ref=window.at[pl.ds(block * leaf_slots + first, size)],
            send_sem=halo_sem.at[0, block // 2],
            recv_sem=halo_sem.at[1, block // 2],
            device_id=(dir_index, near_index + side),
            device_id_type=MESH,
        )

    def start_halo(part):
        first, size = halo_parts[part]
        if size == 0:
            return

        @pl.when(near_index < nears - 1)
        def _():
            halo(1, 0, first, size).start()

        @pl.when(near_index > 0)
        def _():
            halo(-1, 2, first, size).start()

    def radiate_and_send(step, carry):
        tile = flipped(my_tile, tiles - 1 - step, tiles)
        load_rows(step).wait()
        radiate(tile)
        pack(tile, 0)

        @pl.when(step == 0)
        def _():
            all_here()
            start_halo(0)

        for q in range(tile_devices):
            d, n = partner(q)
            d = d + (tile - my_tile) * tile_dirs
            hop(send1[0], recv1[0], d * nears + n, (d, n), 0, 0).start()
        for p in range(1, pieces):
            pack(tile, p)
        return carry

    lax.fori_loop(0, tiles - 1, radiate_and_send, 0)
    load_rows(tiles - 1).wait()
    load_tra.start()
    load_source.start()
    start_pieces(receive, rec_v, load_sem.at[4], 8)
    load_mid.start()
    start_pieces(near_blocks, near_v, load_sem.at[5], 8)
    radiate(my_tile)
    pack(my_tile, 0)
    if tiles == 1:
        all_here()
        start_halo(0)
    for q in range(1, tile_devices):
        d, n = partner(q)
        hop(send1[0], recv1[0], d * nears + n, (d, n), 0, 0).start()
    for p in range(1, pieces):
        pack(my_tile, p)
        start_halo(p)
        for step in range(devices - 1, 0, -1):
            d, n = partner(step)
            hop(send1[p], recv1[p], d * nears + n, (d, n), 0, p).start()

    start_halo(pieces)

    for p in range(pieces):
        recv1[p][me] = send1[p][me]

    load_rec.wait()
    for first, size, _ in chunks:
        total, place = devices * size, 2 * devices * first
        for o in range(total // 128):
            ends = [(i // size) * per + first + i % size for i in (o * 128, o * 128 + 127)]
            low, high = ends[0] // 128 * 128, (ends[1] // 128 + 1) * 128
            row = lax.broadcasted_iota(jnp.int32, (high - low, 128), 0) + low
            column = lax.broadcasted_iota(jnp.int32, (high - low, 128), 1) + o * 128
            owner = (row * (2**16 // per + 1)) >> 16
            inner = row - owner * per - first
            chosen = (inner >= 0) & (inner < size) & (owner * size + inner == column)
            chooser = jnp.where(chosen, 1.0, 0.0).astype(BF16)
            for part in range(2):
                left = rec_v[:, :, pl.ds(part * directions + low, high - low)].reshape(CHILDREN * unknowns, high - low)
                picked = jnp.dot(left, chooser, preferred_element_type=F32).astype(BF16)
                rec_sorted[:, pl.ds(place + part * total + o * 128, 128)] = picked

    load_tra.wait()
    blocks, listed, _, block_size, doubled = tra_v.shape
    per_block = devices // blocks
    for p in range(pieces):
        first, size, padded = chunks[p]
        message = send1[p].shape[1:]
        all_moved(recv1[p], 0, p, 1)
        for b in range(blocks):
            got = recv1[p][pl.ds(b * per_block, per_block)].astype(F32)
            gathered[p][b] = got.reshape(gathered[p].shape[1:])
        for k in range(size):
            for b in range(blocks):
                summed = None
                for l in range(listed):
                    source = source_blocks[b, l] if listing else 0
                    rows_k = gathered[p][source, pl.ds(k, block_size, stride=padded), :]
                    both = jnp.concatenate([rows_k, turned(rows_k)], axis=0).astype(BF16)
                    part = jnp.dot(tra_v[b, l, first + k], both, preferred_element_type=F32)
                    summed = part if summed is None else summed + part
                incoming[p][b, pl.ds(k, block_size, stride=padded), :] = summed
        for b in range(blocks):
            packed = incoming[p][b].reshape((per_block,) + message)
            send2[p][pl.ds(b * per_block, per_block)] = packed.astype(BF16)
        for step in range(devices - 1, 0, -1):
            d, n = partner(step)
            hop(send2[p], recv2[p], d * nears + n, (d, n), 1, p).start()
        recv2[p][me] = send2[p][me]

    load_mid.wait()
    load_near.wait()
    load_source.wait()

    @pl.when(near_index > 0)
    def _():
        halo(1, 0).wait_recv()

    @pl.when(near_index < nears - 1)
    def _():
        halo(-1, 2).wait_recv()

    base = (me - 1) * leaf_slots
    together = 8 if leaf_slots % 8 == 0 else 1

    def nearby(step, carry):
        for u in range(together):
            i = step * together + u
            rows_at = [near_source[e, i] - base for e in range(near_per)]
            sources = [window[jnp.clip(r, 0, 3 * leaf_slots - 1)] for r in rows_at]
            parts = [near_v[i, e] for e in range(near_per)]
            real = jnp.concatenate([p[:, :unknowns] for p in parts], axis=1)
            imag = jnp.concatenate([p[:, unknowns:] for p in parts], axis=1)
            result = jnp.dot(
                jnp.concatenate([real, imag], axis=0),
                jnp.concatenate(sources, axis=0),
                preferred_element_type=F32,
            )
            near_acc[i] = result[:unknowns] + turned(result[unknowns:])
        return carry

    lax.fori_loop(0, leaf_slots // together, nearby, 0)

    def unpack(p):
        first, size, padded = chunks[p]
        total, place = devices * size, 2 * devices * first
        all_moved(recv2[p], 1, p, 1)
        if size % 8:
            spread[p][...] = recv2[p][...].astype(F32).reshape(spread[p].shape)
        for s in range(slots):
            if size % 8:
                for d in range(devices):
                    joined[pl.ds(d * size, size), :] = spread[p][pl.ds((d * slots + s) * padded, size), :]
                values = joined[pl.ds(0, total), :]
            else:
                values = recv2[p][:, s * size // 8 : (s + 1) * size // 8].astype(F32).reshape(total, channels)
            lanes = pl.ds(s * channels, channels)
            fields[pl.ds(place, total), lanes] = values.astype(BF16)
            fields[pl.ds(place + total, total), lanes] = turned(values).astype(BF16)

    group = 4
    height = group * unknowns
    split = 2 * devices * chunks[-1][0]
    rest_depth = 2 * directions - split

    for p in range(pieces - 1):
        unpack(p)
    if pieces > 1:

        def absorb_most(step, carry):
            start = pl.multiple_of(step * height, height)
            far_acc[pl.ds(start, height), :] = jnp.dot(
                rec_sorted[pl.ds(start, height), pl.ds(0, split)],
                fields[pl.ds(0, split), :],
                preferred_element_type=F32,
            )
            return carry

        lax.fori_loop(0, CHILDREN // group, absorb_most, 0)
    unpack(pieces - 1)

    def far_copy(c):
        return pltpu.make_async_remote_copy(
            src_ref=far_send.at[c],
            dst_ref=far_recv.at[c],
            send_sem=far_sem.at[0, c],
            recv_sem=far_sem.at[1, c],
            device_id=(dir_index, mate),
            device_id_type=MESH,
        )

    def absorb(step, carry):
        start = pl.multiple_of(step * height, height)
        far = jnp.dot(
            rec_sorted[pl.ds(start, height), pl.ds(split, rest_depth)],
            fields[pl.ds(split, rest_depth), :],
            preferred_element_type=F32,
        )
        if pieces > 1:
            far = far + far_acc[pl.ds(start, height), :]
        for u in range(group):
            c = step * group + u
            for s in range(slots):
                piece = far[u * unknowns : (u + 1) * unknowns, s * channels : (s + 1) * channels]
                far_own[c, s] = piece
                far_send[c, s] = piece.astype(BF16)
            far_copy(c).start()
        return carry

    lax.fori_loop(0, CHILDREN // group, absorb, 0)

    def finish(c, carry):
        far_copy(c).wait_recv()
        for s in range(parent_slots):
            place = jnp.where(odd == 0, s, even_count + s)
            mine_at = place - half * odd
            mine = (mine_at >= 0) & (mine_at < half)
            own_at = jnp.clip(mine_at, 0, half - 1)
            mate_at = jnp.clip(place - half * (1 - odd), 0, half - 1)
            theirs = far_recv[c, 0]
            for w in range(1, half):
                theirs = jnp.where(mate_at == w, far_recv[c, w], theirs)
            far = jnp.where(mine, far_own[c, own_at], theirs.astype(F32))
            total = far + near_acc[s * CHILDREN + c]
            out[s * CHILDREN + c] = jnp.where(s < own_count, total, 0.0).astype(BF16)
        return carry

    lax.fori_loop(0, CHILDREN, finish, 0)

    to_mate.wait_send()
    for p in range(pieces):
        all_moved(send1[p], 0, p, 0)
        all_moved(send2[p], 1, p, 0)
    for c in range(CHILDREN):
        far_copy(c).wait_send()

    @pl.when(near_index < nears - 1)
    def _():
        halo(1, 0).wait_send()

    @pl.when(near_index > 0)
    def _():
        halo(-1, 2).wait_send()


def body(
    currents, counts, near_source, near_blocks, aggregate, receive, translations, source_blocks
):
    dirs, nears = lax.axis_size("dir"), lax.axis_size("near")
    devices = dirs * nears
    leaf_slots, unknowns, channels = currents.shape
    parent_slots = leaf_slots // CHILDREN
    slots = parent_slots // 2
    blocks, listed, per, block_size, doubled = translations.shape
    directions = aggregate.shape[1]
    chunks = chunks_of(per, slots)
    tiles = 4 if dirs % 4 == 0 and directions % 64 == 0 else 1
    tile_devices = devices // tiles
    lanes = slots * channels
    listing = [source_blocks] if blocks > 1 else []
    hbm_spec = pl.BlockSpec(memory_space=pltpu.HBM)
    messages = [(devices, slots * padded // 8, 8, channels) for _, _, padded in chunks]
    exchange = [pltpu.VMEM(m, BF16) for m in messages]
    boxes = [pltpu.VMEM((blocks, block_size * padded, channels), F32) for _, _, padded in chunks]
    scratch = [
        pltpu.VMEM((leaf_slots + slots * CHILDREN, unknowns, channels), BF16),
        pltpu.VMEM((3 * leaf_slots, unknowns, channels), BF16),
        pltpu.VMEM(near_blocks.shape, BF16),
        pltpu.VMEM(aggregate.shape, BF16),
        pltpu.VMEM(receive.shape, BF16),
        pltpu.VMEM(translations.shape, BF16),
        pltpu.VMEM((2 * CHILDREN * unknowns, lanes), BF16),
        pltpu.VMEM((slots, tile_devices * per, channels), F32),
        pltpu.VMEM((devices * max(size for _, size, _ in chunks), channels), F32),
        pltpu.VMEM((2 * directions, lanes), BF16),
        pltpu.VMEM((CHILDREN * unknowns, 2 * directions), BF16),
        pltpu.VMEM((CHILDREN * unknowns, lanes), F32),
        pltpu.VMEM((CHILDREN, slots, unknowns, channels), F32),
        pltpu.VMEM((CHILDREN, slots, unknowns, channels), BF16),
        pltpu.VMEM((CHILDREN, slots, unknowns, channels), BF16),
        pltpu.VMEM((leaf_slots, unknowns, channels), F32),
        pltpu.SemaphoreType.DMA((6,)),
        pltpu.SemaphoreType.DMA((tiles,)),
        pltpu.SemaphoreType.DMA((2,)),
        pltpu.SemaphoreType.DMA((2, 2)),
        pltpu.SemaphoreType.DMA((2, len(chunks), 2)),
        pltpu.SemaphoreType.DMA((2, CHILDREN)),
        pltpu.SemaphoreType.REGULAR,
        pltpu.SMEM((devices,), jnp.int32),
        pltpu.SMEM((near_blocks.shape[1], leaf_slots), jnp.int32),
        pltpu.SemaphoreType.DMA((2,)),
    ]
    scratch += [pltpu.VMEM((tile_devices * slots * padded, channels), F32) for _, _, padded in chunks]
    scratch += exchange + exchange + boxes + boxes + exchange + exchange
    scratch += [pltpu.VMEM((devices * slots * padded, channels), F32) for _, _, padded in chunks]
    return pl.pallas_call(
        functools.partial(kernel, (dirs, nears, per, slots, chunks, halo_parts_of(leaf_slots, len(chunks)), tiles, blocks > 1)),
        out_shape=jax.ShapeDtypeStruct(currents.shape, BF16),
        in_specs=[pl.BlockSpec(memory_space=pltpu.SMEM)] * len(listing) + [hbm_spec] * 7,
        out_specs=pl.BlockSpec(memory_space=pltpu.VMEM),
        scratch_shapes=scratch,
        compiler_params=pltpu.CompilerParams(
            collective_id=0, has_side_effects=True, vmem_limit_bytes=50 * 2**20
        ),
    )(
        *listing,
        *(
            pltpu.with_memory_space_constraint(array, pltpu.HBM)
            for array in (
                counts,
                near_source.T,
                currents,
                near_blocks,
                aggregate,
                receive,
                translations,
            )
        ),
    )


def solution(mesh):
    return jax.shard_map(
        body,
        mesh=mesh,
        in_specs=(
            P(("dir", "near"), None, None),
            P(),
            P(("dir", "near"), None),
            P(("dir", "near"), None, None, None),
            P(),
            P(),
            P(None, None, ("dir", "near"), None, None),
            P(),
        ),
        out_specs=P(("dir", "near"), None, None),
        check_vma=False,
    )
```

```python
import functools

import jax
import jax.numpy as jnp
from jax import lax
from jax.experimental import pallas as pl
from jax.experimental.pallas import tpu as pltpu
from jax.sharding import PartitionSpec as P

MESH = pl.DeviceIdType.MESH
F32 = jnp.float32
BF16 = jnp.bfloat16
CHILDREN = 8


def turned(values):
    width = values.shape[-1]
    rolled = pltpu.roll(values, width // 2, values.ndim - 1)
    lane = lax.broadcasted_iota(jnp.int32, values.shape, values.ndim - 1)
    return jnp.where(lane < width // 2, -rolled, rolled)


def flipped(index, step, count):
    total = 0
    bit = 1
    while bit < count:
        total = total + bit * lax.rem(index // bit + step // bit, 2)
        bit *= 2
    return total


SHARES = (12, 12, 12)
HALO = (8, 14, 8)


def chunks_of(per, slots):
    sizes = [per * share // sum(SHARES) // 4 * 4 for share in SHARES[:-1]]
    sizes = [size for size in sizes if size]
    sizes.append(per - sum(sizes))
    out, first = [], 0
    for size in sizes:
        out.append((first, size, -(-size * slots // 8) * 8 // slots))
        first += size
    return tuple(out)


def halo_parts_of(leaf_slots, pieces):
    sizes = [HALO[i] * leaf_slots // 32 if i < len(HALO) else 0 for i in range(pieces)]
    sizes.append(leaf_slots - sum(sizes))
    return tuple((sum(sizes[:i]), size) for i, size in enumerate(sizes))


def kernel(dims, *refs):
    dirs, nears, per, slots, chunks, halo_parts, tiles, listing = dims
    devices = dirs * nears
    pieces = len(chunks)
    source_blocks, refs = (refs[0], refs[1:]) if listing else (None, refs)
    counts_hbm, near_source_hbm, currents, near_blocks, aggregate, receive, translations, out = refs[:8]
    scratch = refs[8:]
    (
        pool,
        window,
        near_v,
        agg_v,
        rec_v,
        tra_v,
        stack,
        tile_rows,
        joined,
        fields,
        rec_sorted,
        far_acc,
        far_own,
        far_send,
        far_recv,
        near_acc,
        load_sem,
        agg_sem,
        pair_sem,
        halo_sem,
        a2a_sem,
        far_sem,
        met_sem,
        counts,
        near_source,
        small_sem,
    ) = scratch[:26]
    rest = scratch[26:]
    packs, send1, recv1, gathered, incoming, send2, recv2, spread = (
        rest[i * pieces : (i + 1) * pieces] for i in range(8)
    )
    leaf_slots, unknowns, channels = out.shape
    parent_slots = leaf_slots // CHILDREN
    half = parent_slots // 2
    near_per = near_v.shape[1]
    directions = agg_v.shape[1]
    dir_index = lax.axis_index("dir")
    near_index = lax.axis_index("near")
    me = dir_index * nears + near_index
    odd = lax.rem(near_index, 2)
    mate = near_index + 1 - 2 * odd
    half_leaves = half * CHILDREN
    own = pool.at[pl.ds(0, leaf_slots)]
    borrowed = pool.at[pl.ds(leaf_slots, half_leaves)]

    def deltas(index, count):
        steps, bit = [], 1
        while bit < count:
            steps.append((bit, bit - 2 * bit * lax.rem(index // bit, 2)))
            bit *= 2
        return steps

    dir_deltas, near_deltas = deltas(dir_index, dirs), deltas(near_index, nears)

    def partner(step):
        d, n = dir_index, near_index
        for bit, delta in dir_deltas:
            if step // nears & bit:
                d = d + delta
        for bit, delta in near_deltas:
            if step % nears & bit:
                n = n + delta
        return d, n

    barrier = pltpu.get_barrier_semaphore()

    @pl.when(odd == 0)
    def _():
        pl.semaphore_signal(barrier, inc=1, device_id=(dir_index, mate), device_id_type=MESH)

    load_own = pltpu.make_async_copy(currents, own, load_sem.at[0])
    load_source = pltpu.make_async_copy(near_source_hbm, near_source, small_sem.at[1])
    load_mid = pltpu.make_async_copy(currents, window.at[pl.ds(leaf_slots, leaf_slots)], load_sem.at[2])
    load_tra = pltpu.make_async_copy(translations, tra_v, load_sem.at[3])
    load_rec = pltpu.make_async_copy(receive, rec_v, load_sem.at[4])
    load_near = pltpu.make_async_copy(near_blocks, near_v, load_sem.at[5])

    def start_pieces(source, target, sem, count):
        size = target.shape[0] // count
        for piece in range(count):
            cut = pl.ds(piece * size, size)
            pltpu.make_async_copy(source.at[cut], target.at[cut], sem).start()

    tile_devices = devices // tiles
    tile_dirs = tile_devices // nears
    rows = tile_devices * per
    my_tile = dir_index // tile_dirs

    def load_rows(step):
        tile = flipped(my_tile, tiles - 1 - step, tiles)
        cut = pl.ds(pl.multiple_of(tile * rows, 16), rows)
        return pltpu.make_async_copy(aggregate.at[:, cut, :], agg_v.at[:, cut, :], agg_sem.at[step])

    load_counts = pltpu.make_async_copy(counts_hbm, counts, small_sem.at[0])
    load_counts.start()
    load_own.start()
    for step in range(tiles):
        load_rows(step).start()

    @pl.when(odd == 1)
    def _():
        pl.semaphore_wait(barrier, 1)
        pl.semaphore_signal(met_sem, inc=1, device_id=(dir_index, mate), device_id_type=MESH)

    @pl.when(odd == 0)
    def _():
        pl.semaphore_wait(met_sem, 1)

    to_mate = pltpu.make_async_remote_copy(
        src_ref=currents.at[pl.ds((1 - odd) * half_leaves, half_leaves)],
        dst_ref=borrowed,
        send_sem=pair_sem.at[0],
        recv_sem=pair_sem.at[1],
        device_id=(dir_index, mate),
        device_id_type=MESH,
    )
    to_mate.start()

    @pl.when(odd == 0)
    def _():
        for step in range(devices - 2, 0, -2):
            pl.semaphore_signal(barrier, inc=1, device_id=partner(step), device_id_type=MESH)

    load_counts.wait()
    own_count = counts[me]
    mate_count = counts[dir_index * nears + mate]
    even_count = jnp.where(odd == 0, own_count, mate_count)
    load_own.wait()
    to_mate.wait_recv()
    for w in range(half):
        is_own = jnp.where(odd == 0, w < own_count, half + w >= even_count)
        own_slot = jnp.clip(jnp.where(odd == 0, w, half + w - even_count), 0, parent_slots - 1)
        mate_slot = jnp.clip(jnp.where(odd == 0, w - own_count, w), 0, half - 1)
        slot = jnp.where(is_own, own_slot, parent_slots + mate_slot)
        for c in range(CHILDREN):
            values = pool[slot * CHILDREN + c]
            lanes = pl.ds(w * channels, channels)
            stack[pl.ds(2 * c * unknowns, unknowns), lanes] = values
            stack[pl.ds((2 * c + 1) * unknowns, unknowns), lanes] = turned(values.astype(F32)).astype(BF16)

    def hop(buffer, target, index, to, phase, p):
        return pltpu.make_async_remote_copy(
            src_ref=buffer.at[index],
            dst_ref=target.at[me],
            send_sem=a2a_sem.at[phase, p, 0],
            recv_sem=a2a_sem.at[phase, p, 1],
            device_id=to,
            device_id_type=MESH,
        )

    def all_moved(buffer, phase, p, which):
        some = buffer.at[pl.ds(0, devices - 1)]
        pltpu.make_async_copy(some, some, a2a_sem.at[phase, p, which]).wait()

    def radiate(tile):
        start = pl.multiple_of(tile * rows, 16)
        left = jnp.concatenate([agg_v[c, pl.ds(start, rows), :] for c in range(CHILDREN)], axis=1)
        result = jnp.dot(left, stack[...], preferred_element_type=F32)
        for s in range(slots):
            tile_rows[s] = result[:, s * channels : (s + 1) * channels]

    def pack(tile, p):
        first, size, padded = chunks[p]
        for q in range(tile_devices):
            for s in range(slots):
                packs[p][pl.ds((q * slots + s) * padded, size), :] = tile_rows[s, pl.ds(q * per + first, size), :]
        shape = (tile_devices,) + send1[p].shape[1:]
        send1[p][pl.ds(tile * tile_devices, tile_devices)] = packs[p][...].reshape(shape).astype(BF16)

    def all_here():
        @pl.when(odd == 0)
        def _():
            pl.semaphore_wait(barrier, devices // 2 - 1)
            pl.semaphore_signal(met_sem, inc=1, device_id=(dir_index, mate), device_id_type=MESH)

        @pl.when(odd == 1)
        def _():
            pl.semaphore_wait(met_sem, 1)

    def halo(side, block, first=0, size=None):
        size = leaf_slots if size is None else size
        return pltpu.make_async_remote_copy(
            src_ref=currents.at[pl.ds(first, size)],
            dst_ref=window.at[pl.ds(block * leaf_slots + first, size)],
            send_sem=halo_sem.at[0, block // 2],
            recv_sem=halo_sem.at[1, block // 2],
            device_id=(dir_index, near_index + side),
            device_id_type=MESH,
        )

    def start_halo(part):
        first, size = halo_parts[part]
        if size == 0:
            return

        @pl.when(near_index < nears - 1)
        def _():
            halo(1, 0, first, size).start()

        @pl.when(near_index > 0)
        def _():
            halo(-1, 2, first, size).start()

    def radiate_and_send(step, carry):
        tile = flipped(my_tile, tiles - 1 - step, tiles)
        load_rows(step).wait()
        radiate(tile)
        pack(tile, 0)

        @pl.when(step == 0)
        def _():
            all_here()
            start_halo(0)

        for q in range(tile_devices):
            d, n = partner(q)
            d = d + (tile - my_tile) * tile_dirs
            hop(send1[0], recv1[0], d * nears + n, (d, n), 0, 0).start()
        for p in range(1, pieces):
            pack(tile, p)
        return carry

    lax.fori_loop(0, tiles - 1, radiate_and_send, 0)
    load_rows(tiles - 1).wait()
    load_tra.start()
    load_source.start()
    start_pieces(receive, rec_v, load_sem.at[4], 8)
    load_mid.start()
    start_pieces(near_blocks, near_v, load_sem.at[5], 8)
    radiate(my_tile)
    pack(my_tile, 0)
    if tiles == 1:
        all_here()
        start_halo(0)
    for q in range(1, tile_devices):
        d, n = partner(q)
        hop(send1[0], recv1[0], d * nears + n, (d, n), 0, 0).start()
    for p in range(1, pieces):
        pack(my_tile, p)
        start_halo(p)
        for step in range(devices - 1, 0, -1):
            d, n = partner(step)
            hop(send1[p], recv1[p], d * nears + n, (d, n), 0, p).start()

    start_halo(pieces)

    for p in range(pieces):
        recv1[p][me] = send1[p][me]

    load_rec.wait()
    for first, size, _ in chunks:
        total, place = devices * size, 2 * devices * first
        for o in range(total // 128):
            ends = [(i // size) * per + first + i % size for i in (o * 128, o * 128 + 127)]
            low, high = ends[0] // 128 * 128, (ends[1] // 128 + 1) * 128
            row = lax.broadcasted_iota(jnp.int32, (high - low, 128), 0) + low
            column = lax.broadcasted_iota(jnp.int32, (high - low, 128), 1) + o * 128
            owner = (row * (2**16 // per + 1)) >> 16
            inner = row - owner * per - first
            chosen = (inner >= 0) & (inner < size) & (owner * size + inner == column)
            chooser = jnp.where(chosen, 1.0, 0.0).astype(BF16)
            for part in range(2):
                left = rec_v[:, :, pl.ds(part * directions + low, high - low)].reshape(CHILDREN * unknowns, high - low)
                picked = jnp.dot(left, chooser, preferred_element_type=F32).astype(BF16)
                rec_sorted[:, pl.ds(place + part * total + o * 128, 128)] = picked

    load_tra.wait()
    blocks, listed, _, block_size, doubled = tra_v.shape
    per_block = devices // blocks
    for p in range(pieces):
        first, size, padded = chunks[p]
        message = send1[p].shape[1:]
        all_moved(recv1[p], 0, p, 1)
        for b in range(blocks):
            got = recv1[p][pl.ds(b * per_block, per_block)].astype(F32)
            gathered[p][b] = got.reshape(gathered[p].shape[1:])
        for k in range(size):
            for b in range(blocks):
                summed = None
                for l in range(listed):
                    source = source_blocks[b, l] if listing else 0
                    rows_k = gathered[p][source, pl.ds(k, block_size, stride=padded), :]
                    both = jnp.concatenate([rows_k, turned(rows_k)], axis=0).astype(BF16)
                    part = jnp.dot(tra_v[b, l, first + k], both, preferred_element_type=F32)
                    summed = part if summed is None else summed + part
                incoming[p][b, pl.ds(k, block_size, stride=padded), :] = summed
        for b in range(blocks):
            packed = incoming[p][b].reshape((per_block,) + message)
            send2[p][pl.ds(b * per_block, per_block)] = packed.astype(BF16)
        for step in range(devices - 1, 0, -1):
            d, n = partner(step)
            hop(send2[p], recv2[p], d * nears + n, (d, n), 1, p).start()
        recv2[p][me] = send2[p][me]

    load_mid.wait()
    load_near.wait()
    load_source.wait()

    @pl.when(near_index > 0)
    def _():
        halo(1, 0).wait_recv()

    @pl.when(near_index < nears - 1)
    def _():
        halo(-1, 2).wait_recv()

    base = (me - 1) * leaf_slots
    together = 8 if leaf_slots % 8 == 0 else 1

    def nearby(step, carry):
        for u in range(together):
            i = step * together + u
            rows_at = [near_source[e, i] - base for e in range(near_per)]
            sources = [window[jnp.clip(r, 0, 3 * leaf_slots - 1)] for r in rows_at]
            parts = [near_v[i, e] for e in range(near_per)]
            real = jnp.concatenate([p[:, :unknowns] for p in parts], axis=1)
            imag = jnp.concatenate([p[:, unknowns:] for p in parts], axis=1)
            result = jnp.dot(
                jnp.concatenate([real, imag], axis=0),
                jnp.concatenate(sources, axis=0),
                preferred_element_type=F32,
            )
            near_acc[i] = result[:unknowns] + turned(result[unknowns:])
        return carry

    lax.fori_loop(0, leaf_slots // together, nearby, 0)

    def unpack(p):
        first, size, padded = chunks[p]
        total, place = devices * size, 2 * devices * first
        all_moved(recv2[p], 1, p, 1)
        if size % 8:
            spread[p][...] = recv2[p][...].astype(F32).reshape(spread[p].shape)
        for s in range(slots):
            if size % 8:
                for d in range(devices):
                    joined[pl.ds(d * size, size), :] = spread[p][pl.ds((d * slots + s) * padded, size), :]
                values = joined[pl.ds(0, total), :]
            else:
                values = recv2[p][:, s * size // 8 : (s + 1) * size // 8].astype(F32).reshape(total, channels)
            lanes = pl.ds(s * channels, channels)
            fields[pl.ds(place, total), lanes] = values.astype(BF16)
            fields[pl.ds(place + total, total), lanes] = turned(values).astype(BF16)

    group = 4
    height = group * unknowns
    split = 2 * devices * chunks[-1][0]
    rest_depth = 2 * directions - split

    for p in range(pieces - 1):
        unpack(p)
    if pieces > 1:

        def absorb_most(step, carry):
            start = pl.multiple_of(step * height, height)
            far_acc[pl.ds(start, height), :] = jnp.dot(
                rec_sorted[pl.ds(start, height), pl.ds(0, split)],
                fields[pl.ds(0, split), :],
                preferred_element_type=F32,
            )
            return carry

        lax.fori_loop(0, CHILDREN // group, absorb_most, 0)
    unpack(pieces - 1)

    def far_copy(c):
        return pltpu.make_async_remote_copy(
            src_ref=far_send.at[c],
            dst_ref=far_recv.at[c],
            send_sem=far_sem.at[0, c],
            recv_sem=far_sem.at[1, c],
            device_id=(dir_index, mate),
            device_id_type=MESH,
        )

    def absorb(step, carry):
        start = pl.multiple_of(step * height, height)
        far = jnp.dot(
            rec_sorted[pl.ds(start, height), pl.ds(split, rest_depth)],
            fields[pl.ds(split, rest_depth), :],
            preferred_element_type=F32,
        )
        if pieces > 1:
            far = far + far_acc[pl.ds(start, height), :]
        for u in range(group):
            c = step * group + u
            for s in range(slots):
                piece = far[u * unknowns : (u + 1) * unknowns, s * channels : (s + 1) * channels]
                far_own[c, s] = piece
                far_send[c, s] = piece.astype(BF16)
            far_copy(c).start()
        return carry

    lax.fori_loop(0, CHILDREN // group, absorb, 0)

    def finish(c, carry):
        far_copy(c).wait_recv()
        for s in range(parent_slots):
            place = jnp.where(odd == 0, s, even_count + s)
            mine_at = place - half * odd
            mine = (mine_at >= 0) & (mine_at < half)
            own_at = jnp.clip(mine_at, 0, half - 1)
            mate_at = jnp.clip(place - half * (1 - odd), 0, half - 1)
            theirs = far_recv[c, 0]
            for w in range(1, half):
                theirs = jnp.where(mate_at == w, far_recv[c, w], theirs)
            far = jnp.where(mine, far_own[c, own_at], theirs.astype(F32))
            total = far + near_acc[s * CHILDREN + c]
            out[s * CHILDREN + c] = jnp.where(s < own_count, total, 0.0).astype(BF16)
        return carry

    lax.fori_loop(0, CHILDREN, finish, 0, unroll=True)

    to_mate.wait_send()
    for p in range(pieces):
        all_moved(send1[p], 0, p, 0)
        all_moved(send2[p], 1, p, 0)
    for c in range(CHILDREN):
        far_copy(c).wait_send()

    @pl.when(near_index < nears - 1)
    def _():
        halo(1, 0).wait_send()

    @pl.when(near_index > 0)
    def _():
        halo(-1, 2).wait_send()


def body(
    currents, counts, near_source, near_blocks, aggregate, receive, translations, source_blocks
):
    dirs, nears = lax.axis_size("dir"), lax.axis_size("near")
    devices = dirs * nears
    leaf_slots, unknowns, channels = currents.shape
    parent_slots = leaf_slots // CHILDREN
    slots = parent_slots // 2
    blocks, listed, per, block_size, doubled = translations.shape
    directions = aggregate.shape[1]
    chunks = chunks_of(per, slots)
    tiles = 4 if dirs % 4 == 0 and directions % 64 == 0 else 1
    tile_devices = devices // tiles
    lanes = slots * channels
    listing = [source_blocks] if blocks > 1 else []
    hbm_spec = pl.BlockSpec(memory_space=pltpu.HBM)
    messages = [(devices, slots * padded // 8, 8, channels) for _, _, padded in chunks]
    exchange = [pltpu.VMEM(m, BF16) for m in messages]
    boxes = [pltpu.VMEM((blocks, block_size * padded, channels), F32) for _, _, padded in chunks]
    scratch = [
        pltpu.VMEM((leaf_slots + slots * CHILDREN, unknowns, channels), BF16),
        pltpu.VMEM((3 * leaf_slots, unknowns, channels), BF16),
        pltpu.VMEM(near_blocks.shape, BF16),
        pltpu.VMEM(aggregate.shape, BF16),
        pltpu.VMEM(receive.shape, BF16),
        pltpu.VMEM(translations.shape, BF16),
        pltpu.VMEM((2 * CHILDREN * unknowns, lanes), BF16),
        pltpu.VMEM((slots, tile_devices * per, channels), F32),
        pltpu.VMEM((devices * max(size for _, size, _ in chunks), channels), F32),
        pltpu.VMEM((2 * directions, lanes), BF16),
        pltpu.VMEM((CHILDREN * unknowns, 2 * directions), BF16),
        pltpu.VMEM((CHILDREN * unknowns, lanes), F32),
        pltpu.VMEM((CHILDREN, slots, unknowns, channels), F32),
        pltpu.VMEM((CHILDREN, slots, unknowns, channels), BF16),
        pltpu.VMEM((CHILDREN, slots, unknowns, channels), BF16),
        pltpu.VMEM((leaf_slots, unknowns, channels), F32),
        pltpu.SemaphoreType.DMA((6,)),
        pltpu.SemaphoreType.DMA((tiles,)),
        pltpu.SemaphoreType.DMA((2,)),
        pltpu.SemaphoreType.DMA((2, 2)),
        pltpu.SemaphoreType.DMA((2, len(chunks), 2)),
        pltpu.SemaphoreType.DMA((2, CHILDREN)),
        pltpu.SemaphoreType.REGULAR,
        pltpu.SMEM((devices,), jnp.int32),
        pltpu.SMEM((near_blocks.shape[1], leaf_slots), jnp.int32),
        pltpu.SemaphoreType.DMA((2,)),
    ]
    scratch += [pltpu.VMEM((tile_devices * slots * padded, channels), F32) for _, _, padded in chunks]
    scratch += exchange + exchange + boxes + boxes + exchange + exchange
    scratch += [pltpu.VMEM((devices * slots * padded, channels), F32) for _, _, padded in chunks]
    return pl.pallas_call(
        functools.partial(kernel, (dirs, nears, per, slots, chunks, halo_parts_of(leaf_slots, len(chunks)), tiles, blocks > 1)),
        out_shape=jax.ShapeDtypeStruct(currents.shape, BF16),
        in_specs=[pl.BlockSpec(memory_space=pltpu.SMEM)] * len(listing) + [hbm_spec] * 7,
        out_specs=pl.BlockSpec(memory_space=pltpu.VMEM),
        scratch_shapes=scratch,
        compiler_params=pltpu.CompilerParams(
            collective_id=0, has_side_effects=True, vmem_limit_bytes=50 * 2**20
        ),
    )(
        *listing,
        *(
            pltpu.with_memory_space_constraint(array, pltpu.HBM)
            for array in (
                counts,
                near_source.T,
                currents,
                near_blocks,
                aggregate,
                receive,
                translations,
            )
        ),
    )


def solution(mesh):
    return jax.shard_map(
        body,
        mesh=mesh,
        in_specs=(
            P(("dir", "near"), None, None),
            P(),
            P(("dir", "near"), None),
            P(("dir", "near"), None, None, None),
            P(),
            P(),
            P(None, None, ("dir", "near"), None, None),
            P(),
        ),
        out_specs=P(("dir", "near"), None, None),
        check_vma=False,
    )
```
